32 devices in a mesh: grp: 2 (over x), tok: 4 (over y, core), feat: 4 (over z).
Axes of the slice: x: 2, y: 2, z: 4, core: 2. Of those that a mesh axis runs over, the one named last changes fastest.
Arguments:
- activations: bfloat16 [4096, 3072], P(('grp', 'tok', 'feat')), parts along dimension 0, may hold values from -6 to 6
- block_lists: int32 [2048, 4], P(('grp', 'tok', 'feat')), parts along dimension 0, may hold values from 0 to 15, as said below
- top_positions: int32 [4096, 64], P(('grp', 'tok', 'feat')), parts along dimension 0, may hold values from 0 to 2047, as said below
- enc_weight: bfloat16 [3072, 8192], P(None, ('tok', 'feat')), may hold values from -0.109375 to 0.109375
- enc_bias: float32 [8192], P(('tok', 'feat')), may hold values from -3 to 3
- dec_weight: bfloat16 [8192, 3072], P(('tok', 'feat')), may hold values from -2.5 to 2.5
- dec_bias: float32 [3072], replicated, may hold values from -6 to 6
Outputs:
- enc_grad: bfloat16 [3072, 16384], P(None, ('grp', 'tok', 'feat')), parts along dimension 1
- dec_grad: bfloat16 [16384, 3072], P(('grp', 'tok', 'feat')), parts along dimension 0
The draws below stay inside these ranges and needn't reach their ends.
There are 2 independent parts, one for each index of `grp`. The reference program is written for one: setup_inputs(seed, part) draws one part's arguments, and reference() takes and returns one part's arrays. A program takes and returns all parts, laid end to end along the dimension named above; an argument that names none is the same for every part. Nothing has to cross between parts.
Inputs may be any that keep to these rules, and one draw needn't show every extreme that they name: `block_lists`: each row block names 4 different feature blocks. In the aligned blocks of 64 rows that one device holds, no feature block is named more than 24 times. In every draw one feature block is named exactly 24 times in every such block of rows. `top_positions`: the 64 entries of a token are distinct.
All inputs are finite; a program needn't handle non-finite values.
Results may differ from the reference program's by a relative error of at most 0.0058.
Values may be sent and summed in bfloat16 or wider, within the bound.
A program may use at most 128 MiB of HBM per device.

```python
import math
import jax
import jax.numpy as jnp
from jax import lax

D = 3072
BLOCK = 512
TOPK = 64
NACT = 4
RB = 2
OWNERS = 16
FEATURES = 8192
TOKENS = 2048
RB_DEV = 64
ROWBLOCKS = 1024
SLOTS = 24


def draw_block_lists(key, part):
    tickets = RB_DEV * NACT
    remain = tickets - SLOTS
    lowest = min(SLOTS, max(1, -(-remain // (OWNERS - 1))))
    base_order = jax.random.permutation(jax.random.fold_in(key, 1), OWNERS).astype(jnp.int32)
    hottest = base_order[0]
    others_all = base_order[1:]

    def one_device(dev_key):
        first_key, second_key, third_key, fourth_key = jax.random.split(dev_key, 4)
        shuffled = others_all[jax.random.permutation(first_key, OWNERS - 1)]
        run_length = jax.random.randint(second_key, (OWNERS - 1,), lowest, SLOTS + 1)
        run_ends = jnp.cumsum(run_length)
        ticket_spot = jnp.arange(remain, dtype=jnp.int32)
        run_number = jnp.sum((run_ends[None, :] <= ticket_spot[:, None]).astype(jnp.int32), axis=1)
        sequence = jnp.concatenate([jnp.full((SLOTS,), hottest, jnp.int32), shuffled[run_number].astype(jnp.int32)])
        table = sequence.reshape(NACT, RB_DEV).T
        table = table[jax.random.permutation(third_key, RB_DEV)]
        scores = jax.random.randint(fourth_key, (RB_DEV, NACT), 0, 1 << 20) * NACT + jnp.arange(NACT, dtype=jnp.int32)[None, :]
        col_order = jnp.argsort(scores, axis=1)
        return jnp.take_along_axis(table, col_order, axis=1)
    device_keys = jax.random.split(jax.random.fold_in(key, 2), OWNERS)
    return jax.vmap(one_device)(device_keys).reshape(ROWBLOCKS, NACT).astype(jnp.int32)


def draw_top_positions(key, part):
    candidates = NACT * BLOCK
    scores = jax.random.randint(jax.random.fold_in(key, 3), (TOKENS, candidates), 0, 1 << 16) * candidates + jnp.arange(candidates, dtype=jnp.int32)[None, :]
    return lax.top_k(scores, TOPK)[1].astype(jnp.int32)


def draw_dec_weight(key, part):
    first_key, second_key, third_key = jax.random.split(jax.random.fold_in(key, 4), 3)
    row_scale = jnp.exp(jax.random.uniform(first_key, (FEATURES, 1), jnp.float32) * math.log(10.0))
    col_scale = jnp.exp(jax.random.uniform(second_key, (1, D), jnp.float32) * math.log(10.0))
    entries = jnp.clip(jax.random.normal(third_key, (FEATURES, D), jnp.float32), -4.0, 4.0)
    return (entries * row_scale * col_scale / (20.0 * math.sqrt(TOPK))).astype(jnp.bfloat16)


def level_of(key, shape, cuts, low, top_value):
    level, own = 1.0, jax.random.fold_in(key, 6)
    for axis_at, parts in cuts:
        steps = jnp.exp(jax.random.uniform(jax.random.fold_in(own, axis_at), (parts,), jnp.float32, low / len(cuts), top_value / len(cuts)))
        level = level * jnp.repeat(steps, shape[axis_at] // parts).reshape([-1 if axis == axis_at else 1 for axis in range(len(shape))])
    return level


def normal_values(stream_key, dims, spread, limit, shards=(), held_as=jnp.bfloat16):
    values = spread * jax.random.normal(stream_key, dims, jnp.float32)
    if shards:
        values = values * level_of(stream_key, dims, shards, -0.22, 0.18)
    return jnp.clip(values, -limit, limit).astype(held_as)


def setup_inputs(seed: int = 0, part: int = 0) -> dict:
    streams_of = jax.random.split(jax.random.key(seed), 8)
    part_keys = jax.random.split(jax.random.fold_in(streams_of[7], part), 8)
    activations = normal_values(part_keys[0], (TOKENS, D), 1.0, 6.0, ((0, 16),))
    block_lists = draw_block_lists(jax.random.fold_in(jax.random.fold_in(streams_of[7], part), 71), part)
    top_positions = draw_top_positions(jax.random.fold_in(jax.random.fold_in(streams_of[7], part), 71), part)
    enc_weight = normal_values(streams_of[3], (D, FEATURES), D ** -0.5, 0.109375, ((1, 16),))
    enc_bias = normal_values(streams_of[4], (FEATURES,), 0.5, 3.0, ((0, 16),), jnp.float32)
    dec_weight = draw_dec_weight(jax.random.fold_in(streams_of[7], 71), part)
    dec_bias = normal_values(streams_of[6], (D,), 1.0, 6.0, (), jnp.float32)
    return dict(activations=activations, block_lists=block_lists, top_positions=top_positions, enc_weight=enc_weight, enc_bias=enc_bias, dec_weight=dec_weight, dec_bias=dec_bias)


def routed(owner, block_lists, top_positions):
    rowblock_total = block_lists.shape[0]
    hit_table = (block_lists == owner).astype(jnp.int32)
    member_flag = jnp.sum(hit_table, axis=1).astype(jnp.int32)
    column_index = jnp.argmax(hit_table, axis=1).astype(jnp.int32)
    order_key = (1 - member_flag) * rowblock_total + jnp.arange(rowblock_total, dtype=jnp.int32)
    picked = jnp.argsort(order_key)[: OWNERS * SLOTS].astype(jnp.int32)
    lane_index = jnp.arange(RB, dtype=jnp.int32)
    row_index = (picked[:, None] * RB + lane_index[None, :]).reshape(-1).astype(jnp.int32)
    block_cols = jnp.repeat(column_index[picked], RB)
    valid_flag = jnp.repeat(member_flag[picked], RB)
    offsets = top_positions[row_index] - block_cols[:, None] * BLOCK
    inside = (offsets >= 0) & (offsets < BLOCK) & (valid_flag[:, None] > 0)
    offsets = jnp.where(inside, offsets, BLOCK).astype(jnp.int32)
    slot_total = row_index.shape[0]
    line_index = jnp.arange(slot_total, dtype=jnp.int32)[:, None]
    feat_mask = jnp.zeros((slot_total, BLOCK), jnp.float32).at[line_index, offsets].set(1.0, mode="drop")
    return row_index, feat_mask


def encode(owner, activations, block_lists, top_positions, enc_weight, enc_bias):
    row_index, feat_mask = routed(owner, block_lists, top_positions)
    start = (owner * BLOCK).astype(jnp.int32)
    enc_cols = lax.dynamic_slice_in_dim(enc_weight, start, BLOCK, 1)
    bias_part = lax.dynamic_slice_in_dim(enc_bias, start, BLOCK, 0)
    picked_rows = activations[row_index]
    pre_acts = jnp.dot(picked_rows, enc_cols, preferred_element_type=jnp.float32) + bias_part
    code_vals = (feat_mask * pre_acts).astype(jnp.bfloat16)
    return row_index, feat_mask, picked_rows, code_vals, start


def reference(activations, block_lists, top_positions, enc_weight, enc_bias, dec_weight, dec_bias):
    def add_partial(owner, recon):
        row_index, feat_mask, picked_rows, code_vals, start = encode(owner, activations, block_lists, top_positions, enc_weight, enc_bias)
        dec_rows = lax.dynamic_slice_in_dim(dec_weight, start, BLOCK, 0)
        partial_value = jnp.dot(code_vals, dec_rows, preferred_element_type=jnp.float32).astype(jnp.bfloat16)
        return recon.at[row_index].add(partial_value.astype(jnp.float32))

    recon = lax.fori_loop(0, OWNERS, add_partial, jnp.zeros((TOKENS, D), jnp.float32))
    residual = (recon + dec_bias - activations.astype(jnp.float32)).astype(jnp.bfloat16)

    def gradients(owner):
        row_index, feat_mask, picked_rows, code_vals, start = encode(owner, activations, block_lists, top_positions, enc_weight, enc_bias)
        dec_rows = lax.dynamic_slice_in_dim(dec_weight, start, BLOCK, 0)
        picked_err = residual[row_index]
        grad_codes = lax.dot_general(picked_err, dec_rows, (((1,), (1,)), ((), ())), preferred_element_type=jnp.float32)
        grad_pre = (feat_mask * grad_codes).astype(jnp.bfloat16)
        enc_part = lax.dot_general(picked_rows, grad_pre, (((0,), (0,)), ((), ())), preferred_element_type=jnp.float32).astype(jnp.bfloat16)
        raw_grad = lax.dot_general(code_vals, picked_err, (((0,), (0,)), ((), ())), preferred_element_type=jnp.float32)
        dec_float = dec_rows.astype(jnp.float32)
        along_coef = jnp.sum(raw_grad * dec_float, axis=1) / (jnp.sum(dec_float * dec_float, axis=1) + 1e-6)
        dec_part = (raw_grad - along_coef[:, None] * dec_float).astype(jnp.bfloat16)
        return enc_part, dec_part

    enc_stack, dec_stack = lax.map(gradients, jnp.arange(OWNERS, dtype=jnp.int32))
    enc_grad = jnp.transpose(enc_stack, (1, 0, 2)).reshape(D, FEATURES)
    dec_grad = dec_stack.reshape(FEATURES, D)
    return (enc_grad, dec_grad)
```

```python
import functools

import jax
import jax.numpy as jnp
from jax import lax
from jax.experimental import pallas as pl
from jax.experimental.pallas import tpu as pltpu
from jax.sharding import PartitionSpec as P


def dispatch_rows(send_x, send_rel):
    result = (
        lax.all_to_all(send_x, ("tok", "feat"), split_axis=0, concat_axis=0, tiled=True),
        lax.all_to_all(send_rel, ("tok", "feat"), split_axis=0, concat_axis=0, tiled=True),
    )
    return result


def return_partials(partial_value):
    result = lax.all_to_all(partial_value, ("tok", "feat"), split_axis=0, concat_axis=0, tiled=True)
    return result


def dispatch_errors(send_err):
    result = lax.all_to_all(send_err, ("tok", "feat"), split_axis=0, concat_axis=0, tiled=True)
    return result


def routed_plan(activations, block_lists, top_positions, enc_weight, enc_bias, dec_weight, dec_bias):
    owner_count = lax.axis_size(("tok", "feat"))
    token_count, model_width = activations.shape
    block_rows, active_count = block_lists.shape
    group_rows = token_count // block_rows
    feat_block = enc_weight.shape[1]
    top_count = top_positions.shape[1]
    slot_count = max(2, 3 * token_count * active_count // (2 * group_rows * owner_count))
    per_owner = slot_count * group_rows
    buffer_rows = owner_count * per_owner
    pair_count = block_rows * active_count
    pair_ids = block_lists.reshape(pair_count)
    pair_order = jnp.arange(pair_count, dtype=jnp.int32)
    earlier = (pair_ids[:, None] == pair_ids[None, :]) & (pair_order[None, :] < pair_order[:, None])
    pair_rank = jnp.sum(earlier.astype(jnp.int32), axis=1)
    lane_index = jnp.arange(group_rows, dtype=jnp.int32)
    target = (
        (pair_ids * per_owner + pair_rank * group_rows)[:, None] + lane_index[None, :]
    ).reshape(-1)
    source = ((pair_order // active_count * group_rows)[:, None] + lane_index[None, :]).reshape(-1)
    column = jnp.repeat(pair_order % active_count, group_rows)
    slot_index = jnp.arange(buffer_rows, dtype=jnp.int32)
    hit_bool = slot_index[:, None] == target[None, :]
    hit_float = hit_bool.astype(jnp.float32)
    place_float = jnp.sum(
        hit_float.reshape(buffer_rows, block_rows, active_count, group_rows), axis=2
    ).reshape(buffer_rows, token_count)
    place = place_float.astype(jnp.bfloat16)
    filled = jnp.sum(place_float, axis=1)
    send_x = jnp.dot(place, activations, preferred_element_type=jnp.float32).astype(jnp.bfloat16)
    offsets = top_positions[source] - column[:, None] * feat_block
    offsets = jnp.where((offsets >= 0) & (offsets < feat_block), offsets, feat_block)
    rel_float = (
        jnp.dot(hit_float, offsets.astype(jnp.float32), precision=lax.Precision.HIGHEST)
        + (1.0 - filled)[:, None] * feat_block
    )
    send_rel = rel_float.astype(jnp.int32)
    recv_x, recv_rel = dispatch_rows(
        send_x.reshape(owner_count, per_owner, model_width),
        send_rel.reshape(owner_count, per_owner, top_count),
    )
    recv_x = recv_x.reshape(buffer_rows, model_width)
    recv_rel = recv_rel.reshape(buffer_rows, top_count)
    feature_iota = jnp.arange(feat_block, dtype=jnp.int32)
    mask_bool = jnp.zeros((buffer_rows, feat_block), jnp.bool_)
    for begin in range(0, top_count, 8):
        piece = recv_rel[:, begin : begin + 8]
        mask_bool = mask_bool | jnp.any(piece[:, :, None] == feature_iota[None, None, :], axis=1)
    feat_mask = mask_bool.astype(jnp.float32)
    pre_acts = jnp.dot(recv_x, enc_weight, preferred_element_type=jnp.float32) + enc_bias
    code_vals = (feat_mask * pre_acts).astype(jnp.bfloat16)
    partial_value = jnp.dot(code_vals, dec_weight, preferred_element_type=jnp.float32).astype(
        jnp.bfloat16
    )
    returned = return_partials(partial_value.reshape(owner_count, per_owner, model_width)).reshape(
        buffer_rows, model_width
    )
    summed = lax.dot_general(
        place, returned, (((0,), (0,)), ((), ())), preferred_element_type=jnp.float32
    )
    residual = (summed + dec_bias - activations.astype(jnp.float32)).astype(jnp.bfloat16)
    send_err = jnp.dot(place, residual, preferred_element_type=jnp.float32).astype(jnp.bfloat16)
    recv_err = dispatch_errors(send_err.reshape(owner_count, per_owner, model_width)).reshape(
        buffer_rows, model_width
    )
    grad_codes = lax.dot_general(
        recv_err, dec_weight, (((1,), (1,)), ((), ())), preferred_element_type=jnp.float32
    )
    grad_pre = (feat_mask * grad_codes).astype(jnp.bfloat16)
    enc_grad = lax.dot_general(
        recv_x, grad_pre, (((0,), (0,)), ((), ())), preferred_element_type=jnp.float32
    ).astype(jnp.bfloat16)
    raw_grad = lax.dot_general(
        code_vals, recv_err, (((0,), (0,)), ((), ())), preferred_element_type=jnp.float32
    )
    dec_float = dec_weight.astype(jnp.float32)
    along_coef = jnp.sum(raw_grad * dec_float, axis=1) / (
        jnp.sum(dec_float * dec_float, axis=1) + 1e-06
    )
    dec_grad = (raw_grad - along_coef[:, None] * dec_float).astype(jnp.bfloat16)
    return (enc_grad, dec_grad)


GROUP = ("tok", "feat")


MESH = pl.DeviceIdType.MESH


def route_rows(x, ids, enc_weight, enc_bias, dec_weight, dec_bias, cap, collective_id):
    zs, mates = lax.axis_size("feat"), lax.axis_size("tok")
    rows, width = x.shape
    feat_block = enc_weight.shape[1]
    id_width = ids.shape[1]
    tile = 768
    chunks = width // tile
    block = mates * cap
    away = block - cap
    total, staged = zs * block, zs * away
    bf16, f32 = jnp.bfloat16, jnp.float32
    vmem, hbm = pl.BlockSpec(memory_space=pltpu.VMEM), pl.BlockSpec(memory_space=pl.ANY)
    sem = lambda *lead: pltpu.SemaphoreType.DMA(lead)
    line_sems = [sem(2, zs, chunks), sem(zs, chunks), sem(mates - 1, zs, chunks), sem(mates - 1, zs, chunks)]
    return pl.pallas_call(
        functools.partial(route_kernel, zs, mates, cap),
        out_shape=[
            jax.ShapeDtypeStruct((width, feat_block), bf16),
            jax.ShapeDtypeStruct((feat_block, width), bf16),
        ],
        in_specs=[hbm, vmem, hbm, vmem, hbm, vmem],
        out_specs=[hbm, hbm],
        scratch_shapes=[
            pltpu.VMEM((zs, chunks, rows, tile), bf16),
            pltpu.VMEM((zs, rows, id_width), bf16),
            pltpu.VMEM((chunks, total, tile), bf16),
            pltpu.VMEM((total, id_width), bf16),
            pltpu.VMEM((chunks, staged, tile), bf16),
            pltpu.VMEM((staged, id_width), bf16),
            pltpu.VMEM((zs, rows, block), bf16),
            pltpu.VMEM((zs, block, rows), bf16),
            pltpu.VMEM((total, feat_block), bf16),
            pltpu.VMEM((total, feat_block), bf16),
            pltpu.VMEM((total, feat_block), bf16),
            pltpu.VMEM((chunks, staged, tile), bf16),
            pltpu.VMEM((chunks, total, tile), bf16),
            pltpu.VMEM((zs, chunks, rows, tile), bf16),
            pltpu.VMEM((zs + 1, chunks, rows, tile), bf16),
            pltpu.VMEM((zs, chunks, rows, tile), bf16),
            pltpu.VMEM((chunks, total, tile), bf16),
            pltpu.VMEM((width, feat_block), bf16),
            pltpu.VMEM((chunks, feat_block, tile), bf16),
            pltpu.VMEM((chunks, tile, total), bf16),
            pltpu.VMEM((feat_block, total), bf16),
            pltpu.VMEM((chunks, feat_block, tile), f32),
            pltpu.VMEM((block, feat_block), f32),
        ]
        + line_sems
        + [sem(2, zs), sem(zs), sem(mates - 1, zs), sem(mates - 1, zs)]
        + line_sems
        + [sem(mates - 1, zs, chunks), sem(mates - 1, zs, chunks), sem(zs, chunks), sem(zs + 1, chunks)]
        + [sem(2), sem(chunks), sem(chunks), sem(2, chunks)],
        compiler_params=pltpu.CompilerParams(
            collective_id=collective_id, has_side_effects=True, vmem_limit_bytes=62 * 1024 * 1024
        ),
        name="route_rows",
    )(x, ids, enc_weight, enc_bias.reshape(1, feat_block), dec_weight, dec_bias.reshape(chunks, 1, tile))


def route_kernel(
    zs, mates, cap, x_ref, id_ref, enc_ref, ebias_ref, dec_ref, dbias_ref, enc_out, dec_out,
    x_line, id_line, x_in, id_in, stage, id_stage, spread, pick, codes, hits, grads,
    p_stage, p_in, c_out, c_in, r_line, r_in, enc_v, dec_v, x_turned, codes_turned, raw, found_ref,
    xl_send, xl_recv, xm_send, xm_recv, il_send, il_recv, im_send, im_recv,
    rl_send, rl_recv, rm_send, rm_recv, pm_send, pm_recv, c_send, c_recv,
    once, own_sem, dec_sem, out_sem,
):
    rows, width = x_ref.shape
    chunks, _, tile = dec_v.shape
    feat_block = enc_v.shape[1]
    block, away = mates * cap, (mates - 1) * cap
    tops = id_ref.shape[1] // 2
    parts = feat_block // 256
    bf16, f32 = jnp.bfloat16, jnp.float32
    me, z = lax.axis_index("tok"), lax.axis_index("feat")

    def mate(m):
        return {"tok": lax.rem(me + m + mates, mates)}

    def along(k):
        return {"feat": jnp.minimum(jnp.maximum(z + 1 - 2 * k, 0), zs - 1)}

    def onward(k):
        return (z + 1 - 2 * k >= 0) & (z + 1 - 2 * k < zs)

    def span(zb, size, offset=0, length=None):
        return pl.ds(pl.multiple_of(zb * size + offset, 16), length or size)

    def remote(src, dst, send, recv, where):
        return pltpu.make_async_remote_copy(
            src_ref=src, dst_ref=dst, send_sem=send, recv_sem=recv, device_id=where, device_id_type=MESH
        )

    def line(ref, send, recv, k, zb, j, src=None):
        here = ref.at[zb, j]
        return remote(here if src is None else src, here, send.at[k, zb, j], recv.at[zb, j], along(k))

    def id_hop(k, zb, src=None):
        here = id_line.at[zb]
        return remote(here if src is None else src, here, il_send.at[k, zb], il_recv.at[zb], along(k))

    def id_mate(m, zb):
        return remote(
            id_stage.at[span(zb, away, (m - 1) * cap, cap)], id_in.at[span(zb, block, m * cap, cap)],
            im_send.at[m - 1, zb], im_recv.at[m - 1, zb], mate(m),
        )

    def to_mate(src, dst, send, recv, m, zb, j, sign=1):
        return remote(
            src.at[j, span(zb, away, (m - 1) * cap, cap)], dst.at[j, span(zb, block, m * cap, cap)],
            send.at[m - 1, zb, j], recv.at[m - 1, zb, j], mate(sign * m),
        )

    x_mate = functools.partial(to_mate, stage, x_in, xm_send, xm_recv)
    r_mate = functools.partial(to_mate, stage, r_in, rm_send, rm_recv)
    p_mate = functools.partial(to_mate, p_stage, p_in, pm_send, pm_recv, sign=-1)

    def chain(k, zz, j):
        slot = zz + 1 - k
        return remote(c_out.at[zz, j], c_in.at[slot, j], c_send.at[zz, j], c_recv.at[slot, j], along(k))

    def every(count, body):
        def step(i, carry):
            body(i)
            return carry

        lax.fori_loop(0, count, step, 0)

    def others(body):
        for m in range(1, mates):
            body(m)

    def at_distance(d, body):
        if d == 0:
            body(z, None)
        else:

            def side(k):
                zb = z - d + 2 * d * k
                pl.when((zb >= 0) & (zb < zs))(lambda: body(zb, k))

            every(2, side)

    cols = lambda j: pl.ds(pl.multiple_of(j * tile, tile), tile)
    own_load = lambda j: pltpu.make_async_copy(x_ref.at[:, cols(j)], x_line.at[z, j], own_sem.at[j])
    dec_load = lambda j: pltpu.make_async_copy(dec_ref.at[:, cols(j)], dec_v.at[j], dec_sem.at[j])
    enc_load = pltpu.make_async_copy(enc_ref, enc_v, once.at[0])
    id_load = pltpu.make_async_copy(id_ref, id_line.at[z], once.at[1])
    id_load.start()
    every(chunks, lambda j: own_load(j).start())
    enc_load.start()
    every(chunks, lambda j: dec_load(j).start())
    barrier = pltpu.get_barrier_semaphore()
    others(lambda m: pl.semaphore_signal(barrier, inc=1, device_id=mate(m), device_id_type=MESH))
    for k in range(2):
        pl.when(onward(k))(
            lambda: pl.semaphore_signal(barrier, inc=1, device_id=along(k), device_id_type=MESH)
        )
    pl.semaphore_wait(barrier, mates - 1 + jnp.minimum(z, 1) + jnp.minimum(zs - 1 - z, 1))

    for k in range(2):

        @pl.when(onward(k))
        def _():
            id_hop(k, z, id_ref).start()
            every(chunks, lambda j: line(x_line, xl_send, xl_recv, k, z, j, x_ref.at[:, cols(j)]).start())

    def plan(zb):
        halves = id_line[zb][:, :tops].astype(f32)
        lane = lax.broadcasted_iota(jnp.int32, (rows, block), 1)
        low = lax.broadcasted_iota(jnp.int32, (rows, rows), 0) > lax.broadcasted_iota(jnp.int32, (rows, rows), 1)
        low = jnp.where(low, 1.0, 0.0).astype(bf16)
        named = jnp.zeros((rows, block), f32)
        for m in range(mates):
            owner = lax.rem(me + m, mates) * zs + z
            first = (parts * owner + 1).astype(f32)
            hit = jnp.where((halves >= first) & (halves < first + parts), 1.0, 0.0)
            hit = jnp.max(hit, axis=1, keepdims=True)
            named = jnp.where((lane >= m * cap) & (lane < (m + 1) * cap), hit, named)
        before = jnp.dot(low, named.astype(bf16), preferred_element_type=f32).astype(jnp.int32)
        slot = lax.rem(lane, cap)
        put = jnp.where((before == slot) & (named > 0), 1.0, 0.0)
        spread[zb] = put.astype(bf16)
        pick[zb] = put.T.astype(bf16)

    def picked(zb, values):
        return jnp.dot(pick[zb], values, preferred_element_type=f32).astype(bf16)

    def gather_ids(d):
        def one(zb, k):
            if d == 0:
                id_load.wait()
            else:
                id_hop(k, zb).wait_recv()
                pl.when(onward(k))(lambda: id_hop(k, zb).start())
            plan(zb)
            out = picked(zb, id_line[zb])
            id_in[span(zb, block, 0, cap), :] = out[:cap]
            id_stage[span(zb, away), :] = out[cap:]
            others(lambda m: id_mate(m, zb).start())

        at_distance(d, one)

    def hand_out(ref, dst, send_to, zb, j):
        out = picked(zb, ref[zb, j])
        dst[j, span(zb, block, 0, cap), :] = out[:cap]
        stage[j, span(zb, away), :] = out[cap:]
        others(lambda m: send_to(m, zb, j).start())

    def gather(d, ref, send, recv, dst, send_to):
        def chunk(j):
            def one(zb, k):
                if d > 0:
                    line(ref, send, recv, k, zb, j).wait_recv()
                    pl.when(onward(k))(lambda: line(ref, send, recv, k, zb, j).start())
                else:
                    own_load(j).wait()
                hand_out(ref, dst, send_to, zb, j)

            at_distance(d, one)

        every(chunks, chunk)

    def gather_x(d):
        gather_ids(d)
        gather(d, x_line, xl_send, xl_recv, x_in, x_mate)

    mine = (me * zs + z).astype(f32)
    strip = 16

    def encode(d):
        def one(zb, k):
            others(lambda m: id_mate(m, zb).wait_recv())

            def mark(i):
                entry = id_in[span(zb, block, i * strip, strip), :].astype(f32)
                rel = (entry[:, :tops] - (1.0 + parts * mine)) * 256.0 + entry[:, tops:]
                feature = lax.broadcasted_iota(jnp.int32, (strip, feat_block), 1).astype(f32)
                found = jnp.zeros((strip, feat_block), f32)
                for t in range(tops):
                    found = jnp.where(rel[:, t : t + 1] == feature, 1.0, found)
                found_ref[pl.ds(pl.multiple_of(i * strip, strip), strip), :] = found

            every(block // strip, mark)
            pre = jnp.zeros((block, feat_block), f32)
            for j in range(chunks):
                others(lambda m: x_mate(m, zb, j).wait_recv())
                pre += jnp.dot(
                    x_in[j, span(zb, block), :], enc_v[j * tile : (j + 1) * tile, :], preferred_element_type=f32
                )
            found = found_ref[...]
            code = jnp.where(found > 0, pre + ebias_ref[...], 0.0).astype(bf16)
            codes[span(zb, block), :] = code
            hits[span(zb, block), :] = found.astype(bf16)

            def decode(j):
                part = jnp.dot(codes[span(zb, block), :], dec_v[j], preferred_element_type=f32).astype(bf16)
                p_in[j, span(zb, block, 0, cap), :] = part[:cap]
                p_stage[j, span(zb, away), :] = part[cap:]
                others(lambda m: p_mate(m, zb, j).start())

            every(chunks, decode)

        at_distance(d, one)

    def merged(zz, j):
        others(lambda m: p_mate(m, zz, j).wait_recv())
        return jnp.dot(spread[zz], p_in[j, span(zz, block), :], preferred_element_type=f32)

    def pass_on(i):
        turn = jnp.where(z < zs // 2, 1 + i, zs - 1 - i)
        zz = lax.rem(z + turn, zs)
        k = jnp.where(zz > z, 0, 1)
        first = jnp.where(zz > z, z == 0, z == zs - 1)

        def chunk(j):
            @pl.when(first)
            def _():
                c_out[zz, j] = merged(zz, j).astype(bf16)

            @pl.when(jnp.logical_not(first))
            def _():
                chain(k, zz, j).wait_recv()
                c_out[zz, j] = (merged(zz, j) + c_in[zz + 1 - k, j].astype(f32)).astype(bf16)

            chain(k, zz, j).start()

        every(chunks, chunk)

    def settle(j):
        raw[0, :rows, :] = (
            merged(z, j) + dbias_ref[j] - x_line[z, j].astype(f32)
        )
        for k in range(2):

            @pl.when(onward(1 - k))
            def _():
                chain(k, z, j).wait_recv()
                raw[0, :rows, :] += c_in[z + 1 - k, j].astype(f32)

        r_line[z, j] = raw[0, :rows, :].astype(bf16)
        for k in range(2):
            pl.when(onward(k))(lambda: line(r_line, rl_send, rl_recv, k, z, j).start())
        hand_out(r_line, r_in, r_mate, z, j)

    def gather_r(d):
        gather(d, r_line, rl_send, rl_recv, r_in, r_mate)

    def slopes(d):
        def one(zb, k):
            slope = jnp.zeros((block, feat_block), f32)
            for j in range(chunks):
                others(lambda m: r_mate(m, zb, j).wait_recv())
                slope += lax.dot_general(
                    r_in[j, span(zb, block), :], dec_v[j], (((1,), (1,)), ((), ())), preferred_element_type=f32
                )
            grads[span(zb, block), :] = jnp.where(hits[span(zb, block), :] > 0, slope, 0.0).astype(bf16)

        at_distance(d, one)

    gather_x(0)
    gather_x(1)
    enc_load.wait()
    every(chunks, lambda j: dec_load(j).wait())
    encode(0)
    gather_x(2)
    encode(1)
    gather_x(3)
    encode(2)
    pass_on(0)
    encode(3)
    pass_on(1)
    pass_on(2)
    every(zs, lambda zb: every(chunks, lambda j: others(lambda m: x_mate(m, zb, j).wait_send())))
    every(chunks, settle)
    for j in range(chunks):
        x_turned[j] = x_in[j].T
    codes_turned[...] = codes[...].T
    gather_r(1)
    slopes(0)
    gather_r(2)
    slopes(1)
    gather_r(3)
    slopes(2)
    slopes(3)

    norm = jnp.zeros((feat_block, 1), f32)
    dots = jnp.zeros((feat_block, 1), f32)
    for j in range(chunks):
        value = jnp.dot(codes_turned[...], r_in[j], preferred_element_type=f32)
        raw[j] = value
        dec = dec_v[j].astype(f32)
        norm += jnp.sum(dec * dec, axis=1, keepdims=True)
        dots += jnp.sum(value * dec, axis=1, keepdims=True)
    coef = dots / (norm + 1e-06)
    enc_store = lambda j: pltpu.make_async_copy(
        enc_v.at[pl.ds(j * tile, tile)], enc_out.at[pl.ds(j * tile, tile)], out_sem.at[0, j]
    )
    dec_store = lambda j: pltpu.make_async_copy(dec_v.at[j], dec_out.at[:, pl.ds(j * tile, tile)], out_sem.at[1, j])
    for j in range(chunks):
        dec_v[j] = (raw[j] - coef * dec_v[j].astype(f32)).astype(bf16)
        dec_store(j).start()
    for j in range(chunks):
        enc_v[j * tile : (j + 1) * tile, :] = jnp.dot(
            x_turned[j], grads[...], preferred_element_type=f32
        ).astype(bf16)
        enc_store(j).start()

    def drain(zb):
        def sent(send_line, send_mate, j):
            for k in range(2):
                came = (zb <= z) if k == 0 else (zb >= z)
                pl.when(onward(k) & came)(lambda: send_line(k, zb, j).wait_send())
            if send_mate is not None:
                others(lambda m: send_mate(m, zb, j).wait_send())

        def chunk(j):
            sent(functools.partial(line, x_line, xl_send, xl_recv), None, j)
            sent(functools.partial(line, r_line, rl_send, rl_recv), r_mate, j)
            others(lambda m: p_mate(m, zb, j).wait_send())
            pl.when(zb != z)(lambda: chain(0, zb, j).wait_send())

        every(chunks, chunk)
        for k in range(2):
            came = (zb <= z) if k == 0 else (zb >= z)
            pl.when(onward(k) & came)(lambda: id_hop(k, zb).wait_send())
        others(lambda m: id_mate(m, zb).wait_send())

    every(zs, drain)
    for j in range(chunks):
        dec_store(j).wait()
        enc_store(j).wait()


def id_columns(block_lists, top_positions, feat_block):
    token_count = top_positions.shape[0]
    block_rows, active_count = block_lists.shape
    lists = jnp.repeat(block_lists, token_count // block_rows, axis=0)
    column = top_positions // feat_block
    chosen = jnp.zeros_like(top_positions)
    for k in range(active_count):
        chosen = jnp.where(column == k, lists[:, k : k + 1], chosen)
    within = top_positions % feat_block
    first = chosen * (feat_block // 256) + within // 256 + 1
    return jnp.concatenate([first, within % 256], axis=1).astype(jnp.bfloat16)


def crossed_plan(activations, block_lists, top_positions, enc_weight, enc_bias, dec_weight, dec_bias):
    token_count = activations.shape[0]
    block_rows, active_count = block_lists.shape
    group_rows = token_count // block_rows
    slot_count = max(2, 3 * token_count * active_count // (2 * group_rows * lax.axis_size(GROUP)))
    ids = id_columns(block_lists, top_positions, enc_weight.shape[1])
    enc_grad, dec_grad = route_rows(
        activations, ids, enc_weight, enc_bias, dec_weight, dec_bias, slot_count * group_rows, 1
    )
    return (enc_grad, dec_grad)


def on_device(activations, block_lists, top_positions, *weights):
    rows, width = activations.shape
    feat_block = weights[0].shape[1]
    square = lax.axis_size("tok") == 4 and lax.axis_size("feat") == 4
    even = rows % 128 == 0 and width % 768 == 0 and feat_block % 256 == 0 and 2 * top_positions.shape[1] == 128
    if square and even and lax.axis_size(GROUP) * (feat_block // 256) < 256:
        return crossed_plan(activations, block_lists, top_positions, *weights)
    return routed_plan(activations, block_lists, top_positions, *weights)


def solution(mesh):
    placed = (
        P(("grp", "tok", "feat"), None),
        P(("grp", "tok", "feat"), None),
        P(("grp", "tok", "feat"), None),
        P(None, ("tok", "feat")),
        P(("tok", "feat")),
        P(("tok", "feat"), None),
        P(),
    )
    return jax.shard_map(
        on_device,
        mesh=mesh,
        in_specs=placed,
        out_specs=(P(None, ("grp", "tok", "feat")), P(("grp", "tok", "feat"), None)),
        check_vma=False,
    )
```

```python
import functools

import jax
import jax.numpy as jnp
from jax import lax
from jax.experimental import pallas as pl
from jax.experimental.pallas import tpu as pltpu
from jax.sharding import PartitionSpec as P


def dispatch_rows(send_x, send_rel):
    result = (
        lax.all_to_all(send_x, ("tok", "feat"), split_axis=0, concat_axis=0, tiled=True),
        lax.all_to_all(send_rel, ("tok", "feat"), split_axis=0, concat_axis=0, tiled=True),
    )
    return result


def return_partials(partial_value):
    result = lax.all_to_all(partial_value, ("tok", "feat"), split_axis=0, concat_axis=0, tiled=True)
    return result


def dispatch_errors(send_err):
    result = lax.all_to_all(send_err, ("tok", "feat"), split_axis=0, concat_axis=0, tiled=True)
    return result


def routed_plan(activations, block_lists, top_positions, enc_weight, enc_bias, dec_weight, dec_bias):
    owner_count = lax.axis_size(("tok", "feat"))
    token_count, model_width = activations.shape
    block_rows, active_count = block_lists.shape
    group_rows = token_count // block_rows
    feat_block = enc_weight.shape[1]
    top_count = top_positions.shape[1]
    slot_count = max(2, 3 * token_count * active_count // (2 * group_rows * owner_count))
    per_owner = slot_count * group_rows
    buffer_rows = owner_count * per_owner
    pair_count = block_rows * active_count
    pair_ids = block_lists.reshape(pair_count)
    pair_order = jnp.arange(pair_count, dtype=jnp.int32)
    earlier = (pair_ids[:, None] == pair_ids[None, :]) & (pair_order[None, :] < pair_order[:, None])
    pair_rank = jnp.sum(earlier.astype(jnp.int32), axis=1)
    lane_index = jnp.arange(group_rows, dtype=jnp.int32)
    target = (
        (pair_ids * per_owner + pair_rank * group_rows)[:, None] + lane_index[None, :]
    ).reshape(-1)
    source = ((pair_order // active_count * group_rows)[:, None] + lane_index[None, :]).reshape(-1)
    column = jnp.repeat(pair_order % active_count, group_rows)
    slot_index = jnp.arange(buffer_rows, dtype=jnp.int32)
    hit_bool = slot_index[:, None] == target[None, :]
    hit_float = hit_bool.astype(jnp.float32)
    place_float = jnp.sum(
        hit_float.reshape(buffer_rows, block_rows, active_count, group_rows), axis=2
    ).reshape(buffer_rows, token_count)
    place = place_float.astype(jnp.bfloat16)
    filled = jnp.sum(place_float, axis=1)
    send_x = jnp.dot(place, activations, preferred_element_type=jnp.float32).astype(jnp.bfloat16)
    offsets = top_positions[source] - column[:, None] * feat_block
    offsets = jnp.where((offsets >= 0) & (offsets < feat_block), offsets, feat_block)
    rel_float = (
        jnp.dot(hit_float, offsets.astype(jnp.float32), precision=lax.Precision.HIGHEST)
        + (1.0 - filled)[:, None] * feat_block
    )
    send_rel = rel_float.astype(jnp.int32)
    recv_x, recv_rel = dispatch_rows(
        send_x.reshape(owner_count, per_owner, model_width),
        send_rel.reshape(owner_count, per_owner, top_count),
    )
    recv_x = recv_x.reshape(buffer_rows, model_width)
    recv_rel = recv_rel.reshape(buffer_rows, top_count)
    feature_iota = jnp.arange(feat_block, dtype=jnp.int32)
    mask_bool = jnp.zeros((buffer_rows, feat_block), jnp.bool_)
    for begin in range(0, top_count, 8):
        piece = recv_rel[:, begin : begin + 8]
        mask_bool = mask_bool | jnp.any(piece[:, :, None] == feature_iota[None, None, :], axis=1)
    feat_mask = mask_bool.astype(jnp.float32)
    pre_acts = jnp.dot(recv_x, enc_weight, preferred_element_type=jnp.float32) + enc_bias
    code_vals = (feat_mask * pre_acts).astype(jnp.bfloat16)
    partial_value = jnp.dot(code_vals, dec_weight, preferred_element_type=jnp.float32).astype(
        jnp.bfloat16
    )
    returned = return_partials(partial_value.reshape(owner_count, per_owner, model_width)).reshape(
        buffer_rows, model_width
    )
    summed = lax.dot_general(
        place, returned, (((0,), (0,)), ((), ())), preferred_element_type=jnp.float32
    )
    residual = (summed + dec_bias - activations.astype(jnp.float32)).astype(jnp.bfloat16)
    send_err = jnp.dot(place, residual, preferred_element_type=jnp.float32).astype(jnp.bfloat16)
    recv_err = dispatch_errors(send_err.reshape(owner_count, per_owner, model_width)).reshape(
        buffer_rows, model_width
    )
    grad_codes = lax.dot_general(
        recv_err, dec_weight, (((1,), (1,)), ((), ())), preferred_element_type=jnp.float32
    )
    grad_pre = (feat_mask * grad_codes).astype(jnp.bfloat16)
    enc_grad = lax.dot_general(
        recv_x, grad_pre, (((0,), (0,)), ((), ())), preferred_element_type=jnp.float32
    ).astype(jnp.bfloat16)
    raw_grad = lax.dot_general(
        code_vals, recv_err, (((0,), (0,)), ((), ())), preferred_element_type=jnp.float32
    )
    dec_float = dec_weight.astype(jnp.float32)
    along_coef = jnp.sum(raw_grad * dec_float, axis=1) / (
        jnp.sum(dec_float * dec_float, axis=1) + 1e-06
    )
    dec_grad = (raw_grad - along_coef[:, None] * dec_float).astype(jnp.bfloat16)
    return (enc_grad, dec_grad)


GROUP = ("tok", "feat")


MESH = pl.DeviceIdType.MESH


def route_rows(x, ids, enc_weight, enc_bias, dec_weight, dec_bias, cap, collective_id):
    zs, mates = lax.axis_size("feat"), lax.axis_size("tok")
    rows, width = x.shape
    feat_block = enc_weight.shape[1]
    id_width = ids.shape[1]
    tile = 768
    chunks = width // tile
    block = mates * cap
    away = block - cap
    total, staged = zs * block, zs * away
    bf16, f32 = jnp.bfloat16, jnp.float32
    vmem, hbm = pl.BlockSpec(memory_space=pltpu.VMEM), pl.BlockSpec(memory_space=pl.ANY)
    sem = lambda *lead: pltpu.SemaphoreType.DMA(lead)
    line_sems = [sem(2, zs, chunks), sem(zs, chunks), sem(mates - 1, zs, chunks), sem(mates - 1, zs, chunks)]
    return pl.pallas_call(
        functools.partial(route_kernel, zs, mates, cap),
        out_shape=[
            jax.ShapeDtypeStruct((width, feat_block), bf16),
            jax.ShapeDtypeStruct((feat_block, width), bf16),
        ],
        in_specs=[hbm, vmem, hbm, vmem, hbm, vmem],
        out_specs=[hbm, hbm],
        scratch_shapes=[
            pltpu.VMEM((zs, chunks, rows, tile), bf16),
            pltpu.VMEM((zs, rows, id_width), bf16),
            pltpu.VMEM((chunks, total, tile), bf16),
            pltpu.VMEM((total, id_width), bf16),
            pltpu.VMEM((chunks, staged, tile), bf16),
            pltpu.VMEM((staged, id_width), bf16),
            pltpu.VMEM((zs, rows, block), bf16),
            pltpu.VMEM((zs, block, rows), bf16),
            pltpu.VMEM((total, feat_block), bf16),
            pltpu.VMEM((total, feat_block), bf16),
            pltpu.VMEM((total, feat_block), bf16),
            pltpu.VMEM((chunks, staged, tile), bf16),
            pltpu.VMEM((chunks, total, tile), bf16),
            pltpu.VMEM((zs, chunks, rows, tile), bf16),
            pltpu.VMEM((zs + 1, chunks, rows, tile), bf16),
            pltpu.VMEM((zs, chunks, rows, tile), bf16),
            pltpu.VMEM((chunks, total, tile), bf16),
            pltpu.VMEM((width, feat_block), bf16),
            pltpu.VMEM((chunks, feat_block, tile), bf16),
            pltpu.VMEM((chunks, tile, total), bf16),
            pltpu.VMEM((feat_block, total), bf16),
            pltpu.VMEM((chunks, feat_block, tile), f32),
            pltpu.VMEM((feat_block, 128), f32),
            pltpu.VMEM((feat_block, 128), f32),
            pltpu.VMEM((id_width // 2, 128), f32),
            pltpu.VMEM((feat_block, 128), bf16),
        ]
        + line_sems
        + [sem(zs - 1), sem(zs - 1), sem(mates - 1, zs), sem(mates - 1, zs)]
        + line_sems
        + [sem(mates - 1, zs, chunks), sem(mates - 1, zs, chunks), sem(zs, chunks), sem(zs + 1, chunks)]
        + [sem(2), sem(chunks), sem(chunks), sem(2, chunks)],
        compiler_params=pltpu.CompilerParams(
            collective_id=collective_id, has_side_effects=True, vmem_limit_bytes=62 * 1024 * 1024
        ),
        name="route_rows",
    )(x, ids, enc_weight, enc_bias.reshape(1, feat_block), dec_weight, dec_bias.reshape(chunks, 1, tile))


def route_kernel(
    zs, mates, cap, x_ref, id_ref, enc_ref, ebias_ref, dec_ref, dbias_ref, enc_out, dec_out,
    x_line, id_line, x_in, id_in, stage, id_stage, spread, pick, codes, hits, grads,
    p_stage, p_in, c_out, c_in, r_line, r_in, enc_v, dec_v, x_turned, codes_turned, raw, norm, dots, keys, marks,
    xl_send, xl_recv, xm_send, xm_recv, il_send, il_recv, im_send, im_recv,
    rl_send, rl_recv, rm_send, rm_recv, pm_send, pm_recv, c_send, c_recv,
    once, own_sem, dec_sem, out_sem,
):
    rows, width = x_ref.shape
    chunks, _, tile = dec_v.shape
    feat_block = enc_v.shape[1]
    block, away = mates * cap, (mates - 1) * cap
    tops = id_ref.shape[1] // 2
    parts = feat_block // 256
    bf16, f32 = jnp.bfloat16, jnp.float32
    me, z = lax.axis_index("tok"), lax.axis_index("feat")

    def mate(m):
        return {"tok": lax.rem(me + m + mates, mates)}

    def along(k):
        return {"feat": jnp.minimum(jnp.maximum(z + 1 - 2 * k, 0), zs - 1)}

    def onward(k):
        return (z + 1 - 2 * k >= 0) & (z + 1 - 2 * k < zs)

    def span(zb, size, offset=0, length=None):
        return pl.ds(pl.multiple_of(zb * size + offset, 16), length or size)

    def remote(src, dst, send, recv, where):
        return pltpu.make_async_remote_copy(
            src_ref=src, dst_ref=dst, send_sem=send, recv_sem=recv, device_id=where, device_id_type=MESH
        )

    def line(ref, send, recv, k, zb, j, src=None):
        here = ref.at[zb, j]
        return remote(here if src is None else src, here, send.at[k, zb, j], recv.at[zb, j], along(k))

    def id_send(n):
        return remote(
            id_ref, id_line.at[z], il_send.at[n - 1], il_recv.at[n - 1], {"feat": lax.rem(z + n, zs)}
        )

    def id_mate(m, zb):
        return remote(
            id_stage.at[span(zb, away, (m - 1) * cap, cap)], id_in.at[span(zb, block, m * cap, cap)],
            im_send.at[m - 1, zb], im_recv.at[m - 1, zb], mate(m),
        )

    def to_mate(src, dst, send, recv, m, zb, j, sign=1):
        return remote(
            src.at[j, span(zb, away, (m - 1) * cap, cap)], dst.at[j, span(zb, block, m * cap, cap)],
            send.at[m - 1, zb, j], recv.at[m - 1, zb, j], mate(sign * m),
        )

    x_mate = functools.partial(to_mate, stage, x_in, xm_send, xm_recv)
    r_mate = functools.partial(to_mate, stage, r_in, rm_send, rm_recv)
    p_mate = functools.partial(to_mate, p_stage, p_in, pm_send, pm_recv, sign=-1)

    def chain(k, zz, j):
        slot = zz + 1 - k
        return remote(c_out.at[zz, j], c_in.at[slot, j], c_send.at[zz, j], c_recv.at[slot, j], along(k))

    def every(count, body):
        def step(i, carry):
            body(i)
            return carry

        lax.fori_loop(0, count, step, 0)

    def others(body):
        for m in range(1, mates):
            body(m)

    def at_distance(d, body):
        if d == 0:
            body(z, None)
        else:

            def side(k):
                zb = z - d + 2 * d * k
                pl.when((zb >= 0) & (zb < zs))(lambda: body(zb, k))

            every(2, side)

    cols = lambda j: pl.ds(pl.multiple_of(j * tile, tile), tile)
    own_load = lambda j: pltpu.make_async_copy(x_ref.at[:, cols(j)], x_line.at[z, j], own_sem.at[j])
    dec_load = lambda j: pltpu.make_async_copy(dec_ref.at[:, cols(j)], dec_v.at[j], dec_sem.at[j])
    enc_load = pltpu.make_async_copy(enc_ref, enc_v, once.at[0])
    id_load = pltpu.make_async_copy(id_ref, id_line.at[z], once.at[1])
    id_load.start()
    every(chunks, lambda j: own_load(j).start())
    enc_load.start()
    every(chunks, lambda j: dec_load(j).start())
    barrier = pltpu.get_barrier_semaphore()
    others(lambda m: pl.semaphore_signal(barrier, inc=1, device_id=mate(m), device_id_type=MESH))
    for n in range(1, zs):
        pl.semaphore_signal(barrier, inc=1, device_id={"feat": lax.rem(z + n, zs)}, device_id_type=MESH)
    def plan(zb):
        halves = id_line[zb][:, :tops].astype(f32)
        lane = lax.broadcasted_iota(jnp.int32, (rows, block), 1)
        low = lax.broadcasted_iota(jnp.int32, (rows, rows), 0) > lax.broadcasted_iota(jnp.int32, (rows, rows), 1)
        low = jnp.where(low, 1.0, 0.0).astype(bf16)
        named = jnp.zeros((rows, block), f32)
        for m in range(mates):
            owner = lax.rem(me + m, mates) * zs + z
            first = (parts * owner + 1).astype(f32)
            hit = jnp.where((halves >= first) & (halves < first + parts), 1.0, 0.0)
            hit = jnp.max(hit, axis=1, keepdims=True)
            named = jnp.where((lane >= m * cap) & (lane < (m + 1) * cap), hit, named)
        before = jnp.dot(low, named.astype(bf16), preferred_element_type=f32).astype(jnp.int32)
        slot = lax.rem(lane, cap)
        put = jnp.where((before == slot) & (named > 0), 1.0, 0.0)
        spread[zb] = put.astype(bf16)
        pick[zb] = put.T.astype(bf16)

    def picked(zb, values):
        return jnp.dot(pick[zb], values, preferred_element_type=f32).astype(bf16)

    def share_ids(zb):
        out = picked(zb, id_line[zb])
        id_in[span(zb, block, 0, cap), :] = out[:cap]
        id_stage[span(zb, away), :] = out[cap:]
        others(lambda m: id_mate(m, zb).start())

    def gather_ids():
        def other(n):
            id_send(n).wait_recv()
            zb = lax.rem(z - n + zs, zs)
            plan(zb)
            share_ids(zb)

        for n in range(1, zs):
            other(n)

    def hand_out(ref, dst, send_to, zb, j):
        out = picked(zb, ref[zb, j])
        dst[j, span(zb, block, 0, cap), :] = out[:cap]
        stage[j, span(zb, away), :] = out[cap:]
        others(lambda m: send_to(m, zb, j).start())

    def gather_one(ref, send, recv, dst, send_to, zb, k, j, own=False):
        if not own:
            line(ref, send, recv, k, zb, j).wait_recv()
            pl.when(onward(k))(lambda: line(ref, send, recv, k, zb, j).start())
        hand_out(ref, dst, send_to, zb, j)

    def gather(one, d, begin=0, end=chunks):
        every(end - begin, lambda i: at_distance(d, lambda zb, k: one(zb, k, begin + i)))

    x_one = functools.partial(gather_one, x_line, xl_send, xl_recv, x_in, x_mate)
    r_one = functools.partial(gather_one, r_line, rl_send, rl_recv, r_in, r_mate)
    gather_x, gather_r = functools.partial(gather, x_one), functools.partial(gather, r_one)
    mine = (me * zs + z).astype(f32)
    strip = 64
    half = chunks // 2

    def mark(g):
        at = pl.ds(pl.multiple_of(g * 128, 128), 128)
        turned = id_in[at, :].astype(f32).T
        keys[...] = (turned[:tops] - (1.0 + parts * mine)) * 256.0 + turned[tops:]

        def part(i):
            feature = (lax.broadcasted_iota(jnp.int32, (strip, 128), 0) + i * strip).astype(f32)
            found = jnp.zeros((strip, 128), f32)
            for t in range(tops):
                found = jnp.where(keys[t : t + 1, :] == feature, 1.0, found)
            marks[pl.ds(pl.multiple_of(i * strip, strip), strip), :] = found.astype(bf16)

        every(feat_block // strip, part)
        hits[at, :] = marks[...].T

    def encode(zb):
        pre = jnp.zeros((block, feat_block), f32)
        for j in range(chunks):
            others(lambda m: x_mate(m, zb, j).wait_recv())
            pre += jnp.dot(
                x_in[j, span(zb, block), :], enc_v[j * tile : (j + 1) * tile, :], preferred_element_type=f32
            )
        code = jnp.where(hits[span(zb, block), :] > 0, pre + ebias_ref[...], 0.0).astype(bf16)
        codes[span(zb, block), :] = code

    def decode(zb, h):
        def chunk(i):
            j = h * half + i
            part = jnp.dot(codes[span(zb, block), :], dec_v[j], preferred_element_type=f32).astype(bf16)
            p_in[j, span(zb, block, 0, cap), :] = part[:cap]
            p_stage[j, span(zb, away), :] = part[cap:]
            others(lambda m: p_mate(m, zb, j).start())

        every(half, chunk)

    def merged(zz, j):
        others(lambda m: p_mate(m, zz, j).wait_recv())
        return jnp.dot(spread[zz], p_in[j, span(zz, block), :], preferred_element_type=f32)

    def row_of(i):
        turn = jnp.where(z < zs // 2, 1 + i, zs - 1 - i)
        return lax.rem(z + turn, zs)

    def pass_chunk(i, j):
        zz = row_of(i)
        k = jnp.where(zz > z, 0, 1)
        first = jnp.where(zz > z, z == 0, z == zs - 1)

        @pl.when(first)
        def _():
            c_out[zz, j] = merged(zz, j).astype(bf16)

        @pl.when(jnp.logical_not(first))
        def _():
            chain(k, zz, j).wait_recv()
            c_out[zz, j] = (merged(zz, j) + c_in[zz + 1 - k, j].astype(f32)).astype(bf16)

        chain(k, zz, j).start()

    def pass_on(i, h):
        every(half, lambda c: pass_chunk(i, h * half + c))

    def settle(j):
        raw[0, :rows, :] = (
            merged(z, j) + dbias_ref[j] - x_line[z, j].astype(f32)
        )
        for k in range(2):

            @pl.when(onward(1 - k))
            def _():
                chain(k, z, j).wait_recv()
                raw[0, :rows, :] += c_in[z + 1 - k, j].astype(f32)

        r_line[z, j] = raw[0, :rows, :].astype(bf16)
        for k in range(2):
            pl.when(onward(k))(lambda: line(r_line, rl_send, rl_recv, k, z, j).start())
        hand_out(r_line, r_in, r_mate, z, j)

    def arrived(zb, begin, end):
        every(end - begin, lambda i: others(lambda m: r_mate(m, zb, begin + i).wait_recv()))

    def slopes(zb):
        slope = jnp.zeros((block, feat_block), f32)
        for j in range(chunks):
            slope += lax.dot_general(
                r_in[j, span(zb, block), :], dec_v[j], (((1,), (1,)), ((), ())), preferred_element_type=f32
            )
        grads[span(zb, block), :] = jnp.where(hits[span(zb, block), :] > 0, slope, 0.0).astype(bf16)

    def folded(values):
        return sum(values[:, n * 128 : (n + 1) * 128] for n in range(tile // 128))

    def weigh(j):
        dec = dec_v[j].astype(f32)
        norm[...] += folded(dec * dec)

    def collect(j):
        value = jnp.dot(codes_turned[...], r_in[j], preferred_element_type=f32)
        raw[j] = value
        dots[...] += folded(value * dec_v[j].astype(f32))

    def drain(zb):
        def sent(send_line, send_mate, j):
            for k in range(2):
                came = (zb <= z) if k == 0 else (zb >= z)
                pl.when(onward(k) & came)(lambda: send_line(k, zb, j).wait_send())
            if send_mate is not None:
                others(lambda m: send_mate(m, zb, j).wait_send())

        def chunk(j):
            sent(functools.partial(line, x_line, xl_send, xl_recv), None, j)
            sent(functools.partial(line, r_line, rl_send, rl_recv), r_mate, j)
            others(lambda m: p_mate(m, zb, j).wait_send())
            pl.when(zb != z)(lambda: chain(0, zb, j).wait_send())

        every(chunks, chunk)
        others(lambda m: id_mate(m, zb).wait_send())

    at_end = (z == 0) | (z == zs - 1)
    inside = jnp.logical_not(at_end)

    id_load.wait()
    plan(z)
    pl.semaphore_wait(barrier, mates + zs - 2)
    for n in range(1, zs):
        id_send(n).start()

    for k in range(2):

        @pl.when(onward(k))
        def _():
            every(chunks, lambda j: line(x_line, xl_send, xl_recv, k, z, j, x_ref.at[:, cols(j)]).start())

    share_ids(z)
    def own_x(j):
        own_load(j).wait()
        x_one(z, None, j, own=True)

    every(half, own_x)
    gather_ids()
    every(chunks - half, lambda i: own_x(half + i))
    gather_x(1)
    for m in range(1, mates):
        every(zs, lambda zb: id_mate(m, zb).wait_recv())
    every(zs * block // 128, mark)
    enc_load.wait()
    every(chunks, lambda j: dec_load(j).wait())

    @pl.when(at_end)
    def _():
        gather_x(2, 0, 1)
        encode(row_of(0))
        decode(row_of(0), 0)
        gather_x(2, 1)
        pass_on(0, 0)
        gather_x(3, 0, 1)
        encode(row_of(1))
        decode(row_of(1), 0)
        gather_x(3, 1)
        pass_on(1, 0)
        encode(z)
        decode(z, 0)
        encode(row_of(2))
        decode(row_of(2), 0)

    @pl.when(inside)
    def _():
        gather_x(2)

        def first_half(i):
            zb = row_of(i)
            encode(zb)
            decode(zb, 0)

        every(zs - 1, first_half)
        encode(z)
        decode(z, 0)

    every(zs - 1, lambda i: decode(row_of(i), 1))
    decode(z, 1)
    norm[...] = jnp.zeros(norm.shape, f32)
    dots[...] = jnp.zeros(dots.shape, f32)
    every(chunks, weigh)

    def turn(j):
        x_turned[j] = x_in[j].T

    every(chunks, turn)
    codes_turned[...] = codes[...].T
    every(zs, lambda zb: every(chunks, lambda j: others(lambda m: x_mate(m, zb, j).wait_send())))
    below = z < zs // 2
    inner, inner_way = jnp.where(below, z + 1, z - 1), jnp.where(below, 1, 0)
    outer, outer_way = jnp.where(below, z - 1, z + 1), jnp.where(below, 0, 1)

    @pl.when(at_end)
    def _():
        pass_on(2, 0)
        pass_on(0, 1)
        pass_on(1, 1)
        gather_r(1, 0, half)
        pass_on(2, 1)
        every(half, settle)
        gather_r(2, 0, half)
        gather_r(1, half)
        every(half, lambda i: settle(half + i))
        gather_r(2, half)
        gather_r(3)

    @pl.when(inside)
    def _():
        pass_on(0, 0)
        every(half, settle)
        every(half, lambda i: r_one(inner, inner_way, i))
        pass_on(1, 0)
        pass_on(2, 0)
        pass_on(0, 1)
        pass_on(1, 1)
        every(half, lambda i: settle(half + i))
        pass_on(2, 1)
        every(half, lambda i: r_one(outer, outer_way, i))
        every(half, lambda i: r_one(inner, inner_way, half + i))
        gather_r(2, 0, half)
        every(half, lambda i: r_one(outer, outer_way, half + i))
        gather_r(2, half)

    def near(zb, k):
        arrived(zb, half, chunks)
        slopes(zb)

    every(zs, lambda zb: arrived(zb, 0, half))
    every(half, collect)
    near(z, None)
    at_distance(1, near)
    at_distance(2, near)
    every(zs, drain)
    for n in range(1, zs):
        id_send(n).wait_send()
    at_distance(3, near)
    every(chunks - half, lambda i: collect(half + i))

    coef = jnp.sum(dots[...], axis=1, keepdims=True) / (jnp.sum(norm[...], axis=1, keepdims=True) + 1e-06)
    enc_store = lambda j: pltpu.make_async_copy(
        enc_v.at[pl.ds(j * tile, tile)], enc_out.at[pl.ds(j * tile, tile)], out_sem.at[0, j]
    )
    dec_store = lambda j: pltpu.make_async_copy(dec_v.at[j], dec_out.at[:, pl.ds(j * tile, tile)], out_sem.at[1, j])
    def enc_all(j):
        enc_v[j * tile : (j + 1) * tile, :] = jnp.dot(
            x_turned[j], grads[...], preferred_element_type=f32
        ).astype(bf16)
        enc_store(j).start()

    def dec_all(j):
        dec_v[j] = (raw[j] - coef * dec_v[j].astype(f32)).astype(bf16)
        dec_store(j).start()

    def finish(j):
        dec_store(j).wait()
        enc_store(j).wait()

    [dec_all(j) for j in range(chunks)]
    [enc_all(j) for j in range(chunks)]
    [finish(j) for j in range(chunks)]


def id_columns(block_lists, top_positions, feat_block):
    token_count = top_positions.shape[0]
    block_rows, active_count = block_lists.shape
    lists = jnp.repeat(block_lists, token_count // block_rows, axis=0)
    column = top_positions // feat_block
    chosen = jnp.zeros_like(top_positions)
    for k in range(active_count):
        chosen = jnp.where(column == k, lists[:, k : k + 1], chosen)
    within = top_positions % feat_block
    first = chosen * (feat_block // 256) + within // 256 + 1
    return jnp.concatenate([first, within % 256], axis=1).astype(jnp.bfloat16)


def crossed_plan(activations, block_lists, top_positions, enc_weight, enc_bias, dec_weight, dec_bias):
    token_count = activations.shape[0]
    block_rows, active_count = block_lists.shape
    group_rows = token_count // block_rows
    slot_count = max(2, 3 * token_count * active_count // (2 * group_rows * lax.axis_size(GROUP)))
    ids = id_columns(block_lists, top_positions, enc_weight.shape[1])
    enc_grad, dec_grad = route_rows(
        activations, ids, enc_weight, enc_bias, dec_weight, dec_bias, slot_count * group_rows, 1
    )
    return (enc_grad, dec_grad)


def on_device(activations, block_lists, top_positions, *weights):
    rows, width = activations.shape
    feat_block = weights[0].shape[1]
    square = lax.axis_size("tok") == 4 and lax.axis_size("feat") == 4
    even = rows % 128 == 0 and width % 768 == 0 and feat_block % 256 == 0 and 2 * top_positions.shape[1] == 128
    if square and even and lax.axis_size(GROUP) * (feat_block // 256) < 256:
        return crossed_plan(activations, block_lists, top_positions, *weights)
    return routed_plan(activations, block_lists, top_positions, *weights)


def solution(mesh):
    placed = (
        P(("grp", "tok", "feat"), None),
        P(("grp", "tok", "feat"), None),
        P(("grp", "tok", "feat"), None),
        P(None, ("tok", "feat")),
        P(("tok", "feat")),
        P(("tok", "feat"), None),
        P(),
    )
    return jax.shard_map(
        on_device,
        mesh=mesh,
        in_specs=placed,
        out_specs=(P(None, ("grp", "tok", "feat")), P(("grp", "tok", "feat"), None)),
        check_vma=False,
    )
```

```python
import functools

import jax
import jax.numpy as jnp
from jax import lax
from jax.experimental import pallas as pl
from jax.experimental.pallas import tpu as pltpu
from jax.sharding import PartitionSpec as P


def dispatch_rows(send_x, send_rel):
    result = (
        lax.all_to_all(send_x, ("tok", "feat"), split_axis=0, concat_axis=0, tiled=True),
        lax.all_to_all(send_rel, ("tok", "feat"), split_axis=0, concat_axis=0, tiled=True),
    )
    return result


def return_partials(partial_value):
    result = lax.all_to_all(partial_value, ("tok", "feat"), split_axis=0, concat_axis=0, tiled=True)
    return result


def dispatch_errors(send_err):
    result = lax.all_to_all(send_err, ("tok", "feat"), split_axis=0, concat_axis=0, tiled=True)
    return result


def routed_plan(activations, block_lists, top_positions, enc_weight, enc_bias, dec_weight, dec_bias):
    owner_count = lax.axis_size(("tok", "feat"))
    token_count, model_width = activations.shape
    block_rows, active_count = block_lists.shape
    group_rows = token_count // block_rows
    feat_block = enc_weight.shape[1]
    top_count = top_positions.shape[1]
    slot_count = max(2, 3 * token_count * active_count // (2 * group_rows * owner_count))
    per_owner = slot_count * group_rows
    buffer_rows = owner_count * per_owner
    pair_count = block_rows * active_count
    pair_ids = block_lists.reshape(pair_count)
    pair_order = jnp.arange(pair_count, dtype=jnp.int32)
    earlier = (pair_ids[:, None] == pair_ids[None, :]) & (pair_order[None, :] < pair_order[:, None])
    pair_rank = jnp.sum(earlier.astype(jnp.int32), axis=1)
    lane_index = jnp.arange(group_rows, dtype=jnp.int32)
    target = (
        (pair_ids * per_owner + pair_rank * group_rows)[:, None] + lane_index[None, :]
    ).reshape(-1)
    source = ((pair_order // active_count * group_rows)[:, None] + lane_index[None, :]).reshape(-1)
    column = jnp.repeat(pair_order % active_count, group_rows)
    slot_index = jnp.arange(buffer_rows, dtype=jnp.int32)
    hit_bool = slot_index[:, None] == target[None, :]
    hit_float = hit_bool.astype(jnp.float32)
    place_float = jnp.sum(
        hit_float.reshape(buffer_rows, block_rows, active_count, group_rows), axis=2
    ).reshape(buffer_rows, token_count)
    place = place_float.astype(jnp.bfloat16)
    filled = jnp.sum(place_float, axis=1)
    send_x = jnp.dot(place, activations, preferred_element_type=jnp.float32).astype(jnp.bfloat16)
    offsets = top_positions[source] - column[:, None] * feat_block
    offsets = jnp.where((offsets >= 0) & (offsets < feat_block), offsets, feat_block)
    rel_float = (
        jnp.dot(hit_float, offsets.astype(jnp.float32), precision=lax.Precision.HIGHEST)
        + (1.0 - filled)[:, None] * feat_block
    )
    send_rel = rel_float.astype(jnp.int32)
    recv_x, recv_rel = dispatch_rows(
        send_x.reshape(owner_count, per_owner, model_width),
        send_rel.reshape(owner_count, per_owner, top_count),
    )
    recv_x = recv_x.reshape(buffer_rows, model_width)
    recv_rel = recv_rel.reshape(buffer_rows, top_count)
    feature_iota = jnp.arange(feat_block, dtype=jnp.int32)
    mask_bool = jnp.zeros((buffer_rows, feat_block), jnp.bool_)
    for begin in range(0, top_count, 8):
        piece = recv_rel[:, begin : begin + 8]
        mask_bool = mask_bool | jnp.any(piece[:, :, None] == feature_iota[None, None, :], axis=1)
    feat_mask = mask_bool.astype(jnp.float32)
    pre_acts = jnp.dot(recv_x, enc_weight, preferred_element_type=jnp.float32) + enc_bias
    code_vals = (feat_mask * pre_acts).astype(jnp.bfloat16)
    partial_value = jnp.dot(code_vals, dec_weight, preferred_element_type=jnp.float32).astype(
        jnp.bfloat16
    )
    returned = return_partials(partial_value.reshape(owner_count, per_owner, model_width)).reshape(
        buffer_rows, model_width
    )
    summed = lax.dot_general(
        place, returned, (((0,), (0,)), ((), ())), preferred_element_type=jnp.float32
    )
    residual = (summed + dec_bias - activations.astype(jnp.float32)).astype(jnp.bfloat16)
    send_err = jnp.dot(place, residual, preferred_element_type=jnp.float32).astype(jnp.bfloat16)
    recv_err = dispatch_errors(send_err.reshape(owner_count, per_owner, model_width)).reshape(
        buffer_rows, model_width
    )
    grad_codes = lax.dot_general(
        recv_err, dec_weight, (((1,), (1,)), ((), ())), preferred_element_type=jnp.float32
    )
    grad_pre = (feat_mask * grad_codes).astype(jnp.bfloat16)
    enc_grad = lax.dot_general(
        recv_x, grad_pre, (((0,), (0,)), ((), ())), preferred_element_type=jnp.float32
    ).astype(jnp.bfloat16)
    raw_grad = lax.dot_general(
        code_vals, recv_err, (((0,), (0,)), ((), ())), preferred_element_type=jnp.float32
    )
    dec_float = dec_weight.astype(jnp.float32)
    along_coef = jnp.sum(raw_grad * dec_float, axis=1) / (
        jnp.sum(dec_float * dec_float, axis=1) + 1e-06
    )
    dec_grad = (raw_grad - along_coef[:, None] * dec_float).astype(jnp.bfloat16)
    return (enc_grad, dec_grad)


GROUP = ("tok", "feat")


MESH = pl.DeviceIdType.MESH


def route_rows(x, positions, lists, enc_weight, enc_bias, dec_weight, dec_bias, cap, tile, early, collective_id):
    zs, mates = lax.axis_size("feat"), lax.axis_size("tok")
    rows, width = x.shape
    feat_block = enc_weight.shape[1]
    id_width = 2 * positions.shape[0]
    chunks = width // tile
    block = mates * cap
    away = block - cap
    total, staged = zs * block, zs * away
    bf16, f32 = jnp.bfloat16, jnp.float32
    vmem, hbm = pl.BlockSpec(memory_space=pltpu.VMEM), pl.BlockSpec(memory_space=pl.ANY)
    sem = lambda *lead: pltpu.SemaphoreType.DMA(lead)
    line_sems = [sem(2, zs, chunks), sem(zs, chunks), sem(mates - 1, zs, chunks), sem(mates - 1, zs, chunks)]
    return pl.pallas_call(
        functools.partial(route_kernel, zs, mates, cap, early),
        out_shape=[
            jax.ShapeDtypeStruct((width, feat_block), bf16),
            jax.ShapeDtypeStruct((feat_block, width), bf16),
        ],
        in_specs=[hbm, vmem, vmem, hbm, vmem, hbm, vmem],
        out_specs=[hbm, hbm],
        scratch_shapes=[
            pltpu.VMEM((zs, chunks, rows, tile), bf16),
            pltpu.VMEM((zs, rows, id_width), bf16),
            pltpu.VMEM((chunks, total, tile), bf16),
            pltpu.VMEM((total, id_width), bf16),
            pltpu.VMEM((chunks, staged, tile), bf16),
            pltpu.VMEM((staged, id_width), bf16),
            pltpu.VMEM((zs, rows, block), bf16),
            pltpu.VMEM((zs, block, rows), bf16),
            pltpu.VMEM((total, feat_block), bf16),
            pltpu.VMEM((total, feat_block), bf16),
            pltpu.VMEM((total, feat_block), bf16),
            pltpu.VMEM((chunks, staged, tile), bf16),
            pltpu.VMEM((chunks, total, tile), bf16),
            pltpu.VMEM((zs, chunks, rows, tile), bf16),
            pltpu.VMEM((zs + 1, chunks, rows, tile), bf16),
            pltpu.VMEM((zs, chunks, rows, tile), bf16),
            pltpu.VMEM((chunks, total, tile), bf16),
            pltpu.VMEM((width, feat_block), bf16),
            pltpu.VMEM((chunks, feat_block, tile), bf16),
            pltpu.VMEM((chunks, tile, total), bf16),
            pltpu.VMEM((feat_block, total), bf16),
            pltpu.VMEM((chunks, feat_block, tile), f32),
            pltpu.VMEM((feat_block, 128), f32),
            pltpu.VMEM((feat_block, 128), f32),
            pltpu.VMEM((id_width // 2, 128), f32),
            pltpu.VMEM((feat_block, 128), bf16),
        ]
        + line_sems
        + [sem(zs - 1), sem(zs - 1), sem(mates - 1, zs), sem(mates - 1, zs)]
        + line_sems
        + [sem(mates - 1, zs, chunks), sem(mates - 1, zs, chunks), sem(zs, chunks), sem(zs + 1, chunks)]
        + [sem(1), sem(chunks), sem(chunks), sem(2, chunks)],
        compiler_params=pltpu.CompilerParams(
            collective_id=collective_id, has_side_effects=True, vmem_limit_bytes=62 * 1024 * 1024
        ),
        name="route_rows",
    )(x, positions, lists, enc_weight, enc_bias.reshape(1, feat_block), dec_weight, dec_bias.reshape(chunks, 1, tile))


def route_kernel(
    zs, mates, cap, early, x_ref, position_ref, list_ref, enc_ref, ebias_ref, dec_ref, dbias_ref, enc_out, dec_out,
    x_line, id_line, x_in, id_in, stage, id_stage, spread, pick, codes, hits, grads,
    p_stage, p_in, c_out, c_in, r_line, r_in, enc_v, dec_v, x_turned, codes_turned, raw, norm, dots, keys, marks,
    xl_send, xl_recv, xm_send, xm_recv, il_send, il_recv, im_send, im_recv,
    rl_send, rl_recv, rm_send, rm_recv, pm_send, pm_recv, c_send, c_recv,
    once, own_sem, dec_sem, out_sem,
):
    rows, width = x_ref.shape
    chunks, _, tile = dec_v.shape
    feat_block = enc_v.shape[1]
    block, away = mates * cap, (mates - 1) * cap
    tops = position_ref.shape[0]
    parts = feat_block // 256
    bf16, f32 = jnp.bfloat16, jnp.float32
    me, z = lax.axis_index("tok"), lax.axis_index("feat")

    def mate(m):
        return {"tok": lax.rem(me + m + mates, mates)}

    def along(k):
        return {"feat": jnp.minimum(jnp.maximum(z + 1 - 2 * k, 0), zs - 1)}

    def onward(k):
        return (z + 1 - 2 * k >= 0) & (z + 1 - 2 * k < zs)

    def span(zb, size, offset=0, length=None):
        return pl.ds(pl.multiple_of(zb * size + offset, 16), length or size)

    def remote(src, dst, send, recv, where):
        return pltpu.make_async_remote_copy(
            src_ref=src, dst_ref=dst, send_sem=send, recv_sem=recv, device_id=where, device_id_type=MESH
        )

    def line(ref, send, recv, k, zb, j, src=None):
        here = ref.at[zb, j]
        return remote(here if src is None else src, here, send.at[k, zb, j], recv.at[zb, j], along(k))

    def id_send(n):
        return remote(
            id_line.at[z], id_line.at[z], il_send.at[n - 1], il_recv.at[n - 1], {"feat": lax.rem(z + n, zs)}
        )

    def id_mate(m, zb):
        return remote(
            id_stage.at[span(zb, away, (m - 1) * cap, cap)], id_in.at[span(zb, block, m * cap, cap)],
            im_send.at[m - 1, zb], im_recv.at[m - 1, zb], mate(m),
        )

    def to_mate(src, dst, send, recv, m, zb, j, sign=1):
        return remote(
            src.at[j, span(zb, away, (m - 1) * cap, cap)], dst.at[j, span(zb, block, m * cap, cap)],
            send.at[m - 1, zb, j], recv.at[m - 1, zb, j], mate(sign * m),
        )

    x_mate = functools.partial(to_mate, stage, x_in, xm_send, xm_recv)
    r_mate = functools.partial(to_mate, stage, r_in, rm_send, rm_recv)
    p_mate = functools.partial(to_mate, p_stage, p_in, pm_send, pm_recv, sign=-1)

    def chain(k, zz, j):
        slot = zz + 1 - k
        return remote(c_out.at[zz, j], c_in.at[slot, j], c_send.at[zz, j], c_recv.at[slot, j], along(k))

    def every(count, body):
        def step(i, carry):
            body(i)
            return carry

        lax.fori_loop(0, count, step, 0)

    def others(body):
        for m in range(1, mates):
            body(m)

    def at_distance(d, body):
        if d == 0:
            body(z, None)
        else:

            def side(k):
                zb = z - d + 2 * d * k
                pl.when((zb >= 0) & (zb < zs))(lambda: body(zb, k))

            every(2, side)

    cols = lambda j: pl.ds(pl.multiple_of(j * tile, tile), tile)
    own_load = lambda j: pltpu.make_async_copy(x_ref.at[:, cols(j)], x_line.at[z, j], own_sem.at[j])
    dec_load = lambda j: pltpu.make_async_copy(dec_ref.at[:, cols(j)], dec_v.at[j], dec_sem.at[j])
    enc_load = pltpu.make_async_copy(enc_ref, enc_v, once.at[0])
    every(chunks, lambda j: own_load(j).start())
    enc_load.start()
    every(chunks, lambda j: dec_load(j).start())
    barrier = pltpu.get_barrier_semaphore()
    others(lambda m: pl.semaphore_signal(barrier, inc=1, device_id=mate(m), device_id_type=MESH))
    for n in range(1, zs):
        pl.semaphore_signal(barrier, inc=1, device_id={"feat": lax.rem(z + n, zs)}, device_id_type=MESH)
    def plan(zb):
        halves = id_line[zb][:, :tops].astype(f32)
        lane = lax.broadcasted_iota(jnp.int32, (rows, block), 1)
        low = lax.broadcasted_iota(jnp.int32, (rows, rows), 0) > lax.broadcasted_iota(jnp.int32, (rows, rows), 1)
        low = jnp.where(low, 1.0, 0.0).astype(bf16)
        named = jnp.zeros((rows, block), f32)
        for m in range(mates):
            owner = lax.rem(me + m, mates) * zs + z
            first = (parts * owner + 1).astype(f32)
            hit = jnp.where((halves >= first) & (halves < first + parts), 1.0, 0.0)
            hit = jnp.max(hit, axis=1, keepdims=True)
            named = jnp.where((lane >= m * cap) & (lane < (m + 1) * cap), hit, named)
        before = jnp.dot(low, named.astype(bf16), preferred_element_type=f32).astype(jnp.int32)
        slot = lax.rem(lane, cap)
        put = jnp.where((before == slot) & (named > 0), 1.0, 0.0)
        spread[zb] = put.astype(bf16)
        pick[zb] = put.T.astype(bf16)

    def picked(zb, values):
        return jnp.dot(pick[zb], values, preferred_element_type=f32).astype(bf16)

    def share_ids(zb):
        out = picked(zb, id_line[zb])
        id_in[span(zb, block, 0, cap), :] = out[:cap]
        id_stage[span(zb, away), :] = out[cap:]
        others(lambda m: id_mate(m, zb).start())

    def gather_ids():
        def other(n):
            id_send(n).wait_recv()
            zb = lax.rem(z - n + zs, zs)
            plan(zb)
            share_ids(zb)

        for n in range(1, zs):
            other(n)

    def hand_out(ref, dst, send_to, zb, j):
        out = picked(zb, ref[zb, j])
        dst[j, span(zb, block, 0, cap), :] = out[:cap]
        stage[j, span(zb, away), :] = out[cap:]
        others(lambda m: send_to(m, zb, j).start())

    def gather_one(ref, send, recv, dst, send_to, zb, k, j, own=False):
        if not own:
            line(ref, send, recv, k, zb, j).wait_recv()
            pl.when(onward(k))(lambda: line(ref, send, recv, k, zb, j).start())
        hand_out(ref, dst, send_to, zb, j)

    def gather(one, d, begin=0, end=chunks):
        every(end - begin, lambda i: at_distance(d, lambda zb, k: one(zb, k, begin + i)))

    x_one = functools.partial(gather_one, x_line, xl_send, xl_recv, x_in, x_mate)
    r_one = functools.partial(gather_one, r_line, rl_send, rl_recv, r_in, r_mate)
    gather_x, gather_r = functools.partial(gather, x_one), functools.partial(gather, r_one)
    mine = (me * zs + z).astype(f32)
    strip = 64
    late = chunks - early

    def mark(g):
        at = pl.ds(pl.multiple_of(g * 128, 128), 128)
        turned = id_in[at, :].astype(f32).T
        keys[...] = (turned[:tops] - (1.0 + parts * mine)) * 256.0 + turned[tops:]

        def part(i):
            feature = (lax.broadcasted_iota(jnp.int32, (strip, 128), 0) + i * strip).astype(f32)
            found = jnp.zeros((strip, 128), f32)
            for t in range(tops):
                found = jnp.where(keys[t : t + 1, :] == feature, 1.0, found)
            marks[pl.ds(pl.multiple_of(i * strip, strip), strip), :] = found.astype(bf16)

        every(feat_block // strip, part)
        hits[at, :] = marks[...].T

    def encode(zb):
        pre = jnp.zeros((block, feat_block), f32)
        for j in range(chunks):
            others(lambda m: x_mate(m, zb, j).wait_recv())
            pre += jnp.dot(
                x_in[j, span(zb, block), :], enc_v[j * tile : (j + 1) * tile, :], preferred_element_type=f32
            )
        code = jnp.where(hits[span(zb, block), :] > 0, pre + ebias_ref[...], 0.0).astype(bf16)
        codes[span(zb, block), :] = code

    def decode(zb, part):
        def chunk(i):
            j = part * early + i
            out = jnp.dot(codes[span(zb, block), :], dec_v[j], preferred_element_type=f32).astype(bf16)
            p_in[j, span(zb, block, 0, cap), :] = out[:cap]
            p_stage[j, span(zb, away), :] = out[cap:]
            others(lambda m: p_mate(m, zb, j).start())

        every(late if part else early, chunk)

    def merged(zz, j):
        others(lambda m: p_mate(m, zz, j).wait_recv())
        return jnp.dot(spread[zz], p_in[j, span(zz, block), :], preferred_element_type=f32)

    def row_of(i):
        turn = jnp.where(z < zs // 2, 1 + i, zs - 1 - i)
        return lax.rem(z + turn, zs)

    def pass_chunk(i, j):
        zz = row_of(i)
        k = jnp.where(zz > z, 0, 1)
        first = jnp.where(zz > z, z == 0, z == zs - 1)

        @pl.when(first)
        def _():
            c_out[zz, j] = merged(zz, j).astype(bf16)

        @pl.when(jnp.logical_not(first))
        def _():
            chain(k, zz, j).wait_recv()
            c_out[zz, j] = (merged(zz, j) + c_in[zz + 1 - k, j].astype(f32)).astype(bf16)

        chain(k, zz, j).start()

    def pass_on(i, part):
        every(late if part else early, lambda c: pass_chunk(i, part * early + c))

    def settle(j):
        raw[0, :rows, :] = (
            merged(z, j) + dbias_ref[j] - x_line[z, j].astype(f32)
        )
        for k in range(2):

            @pl.when(onward(1 - k))
            def _():
                chain(k, z, j).wait_recv()
                raw[0, :rows, :] += c_in[z + 1 - k, j].astype(f32)

        r_line[z, j] = raw[0, :rows, :].astype(bf16)
        for k in range(2):
            pl.when(onward(k))(lambda: line(r_line, rl_send, rl_recv, k, z, j).start())
        hand_out(r_line, r_in, r_mate, z, j)

    def arrived(zb, begin, end):
        every(end - begin, lambda i: others(lambda m: r_mate(m, zb, begin + i).wait_recv()))

    def slopes(zb):
        slope = jnp.zeros((block, feat_block), f32)
        for j in range(chunks):
            slope += lax.dot_general(
                r_in[j, span(zb, block), :], dec_v[j], (((1,), (1,)), ((), ())), preferred_element_type=f32
            )
        grads[span(zb, block), :] = jnp.where(hits[span(zb, block), :] > 0, slope, 0.0).astype(bf16)

    def folded(values):
        return sum(values[:, n * 128 : (n + 1) * 128] for n in range(tile // 128))

    def weigh(j):
        dec = dec_v[j].astype(f32)
        norm[...] += folded(dec * dec)

    def collect(j):
        value = jnp.dot(codes_turned[...], r_in[j], preferred_element_type=f32)
        raw[j] = value
        dots[...] += folded(value * dec_v[j].astype(f32))

    def drain(zb):
        def sent(send_line, send_mate, j):
            for k in range(2):
                came = (zb <= z) if k == 0 else (zb >= z)
                pl.when(onward(k) & came)(lambda: send_line(k, zb, j).wait_send())
            if send_mate is not None:
                others(lambda m: send_mate(m, zb, j).wait_send())

        def chunk(j):
            sent(functools.partial(line, x_line, xl_send, xl_recv), None, j)
            sent(functools.partial(line, r_line, rl_send, rl_recv), r_mate, j)
            others(lambda m: p_mate(m, zb, j).wait_send())
            pl.when(zb != z)(lambda: chain(0, zb, j).wait_send())

        every(chunks, chunk)
        others(lambda m: id_mate(m, zb).wait_send())

    at_end = (z == 0) | (z == zs - 1)
    inside = jnp.logical_not(at_end)

    def own_ids():
        groups = list_ref.shape[1]
        token = lax.broadcasted_iota(jnp.int32, (groups, rows), 1) // (rows // groups)
        wide = jnp.where(token == lax.broadcasted_iota(jnp.int32, (groups, rows), 0), 1.0, 0.0).astype(bf16)
        lists = jnp.dot(list_ref[...].astype(f32).astype(bf16), wide, preferred_element_type=f32)
        position = position_ref[...]
        column, within = position // feat_block, position % feat_block
        chosen = jnp.zeros((tops, rows), f32)
        for k in range(list_ref.shape[0]):
            chosen = jnp.where(column == k, lists[k : k + 1, :], chosen)
        first = chosen * parts + (within // 256 + 1).astype(f32)
        pair = jnp.concatenate([first, (within % 256).astype(f32)], axis=0)
        id_line[z] = pair.T.astype(bf16)

    own_ids()
    plan(z)
    pl.semaphore_wait(barrier, mates + zs - 2)
    for n in range(1, zs):
        id_send(n).start()

    for k in range(2):

        @pl.when(onward(k))
        def _():
            every(chunks, lambda j: line(x_line, xl_send, xl_recv, k, z, j, x_ref.at[:, cols(j)]).start())

    share_ids(z)
    def own_x(j):
        own_load(j).wait()
        x_one(z, None, j, own=True)

    every(early, own_x)
    gather_ids()
    every(late, lambda i: own_x(early + i))
    gather_x(1)
    for m in range(1, mates):
        every(zs, lambda zb: id_mate(m, zb).wait_recv())
    every(zs * block // 128, mark)
    enc_load.wait()
    every(chunks, lambda j: dec_load(j).wait())

    @pl.when(at_end)
    def _():
        gather_x(2, 0, 1)
        encode(row_of(0))
        decode(row_of(0), 0)
        gather_x(2, 1)
        pass_on(0, 0)
        gather_x(3, 0, 1)
        encode(row_of(1))
        decode(row_of(1), 0)
        gather_x(3, 1)
        pass_on(1, 0)
        encode(z)
        decode(z, 0)
        encode(row_of(2))
        decode(row_of(2), 0)

    @pl.when(inside)
    def _():
        gather_x(2)

        encode(row_of(0))
        decode(row_of(0), 0)
        encode(z)
        decode(z, 0)
        encode(row_of(1))
        decode(row_of(1), 0)
        encode(row_of(2))
        decode(row_of(2), 0)

    @pl.when(at_end)
    def _():
        decode(row_of(0), 1)
        decode(row_of(1), 1)
        decode(row_of(2), 1)
        decode(z, 1)

    @pl.when(inside)
    def _():
        decode(row_of(0), 1)
        decode(z, 1)
        decode(row_of(1), 1)
        decode(row_of(2), 1)

    norm[...] = jnp.zeros(norm.shape, f32)
    dots[...] = jnp.zeros(dots.shape, f32)
    every(chunks, weigh)

    def turn(j):
        x_turned[j] = x_in[j].T

    every(chunks, turn)
    codes_turned[...] = codes[...].T
    every(zs, lambda zb: every(chunks, lambda j: others(lambda m: x_mate(m, zb, j).wait_send())))
    below = z < zs // 2
    inner, inner_way = jnp.where(below, z + 1, z - 1), jnp.where(below, 1, 0)
    outer, outer_way = jnp.where(below, z - 1, z + 1), jnp.where(below, 0, 1)

    @pl.when(at_end)
    def _():
        pass_on(2, 0)
        pass_on(0, 1)
        pass_on(1, 1)
        gather_r(1, 0, early)
        pass_on(2, 1)
        every(early, settle)
        gather_r(2, 0, early)
        gather_r(1, early)
        every(late, lambda i: settle(early + i))
        gather_r(2, early)
        gather_r(3)

    @pl.when(inside)
    def _():
        pass_on(0, 0)
        every(early, settle)
        every(early, lambda i: r_one(inner, inner_way, i))
        pass_on(1, 0)
        pass_on(2, 0)
        pass_on(0, 1)
        pass_on(1, 1)
        every(late, lambda i: settle(early + i))
        pass_on(2, 1)
        every(early, lambda i: r_one(outer, outer_way, i))
        every(late, lambda i: r_one(inner, inner_way, early + i))
        gather_r(2, 0, early)
        every(late, lambda i: r_one(outer, outer_way, early + i))
        gather_r(2, early)

    last = jnp.where(at_end, row_of(2), row_of(1))

    def whole(zb):
        arrived(zb, 0, chunks)
        slopes(zb)

    whole(z)
    whole(row_of(0))
    whole(jnp.where(at_end, row_of(1), row_of(2)))
    slope = jnp.zeros((block, feat_block), f32)
    for j in range(chunks):
        arrived(last, j, j + 1)
        slope += lax.dot_general(
            r_in[j, span(last, block), :], dec_v[j], (((1,), (1,)), ((), ())), preferred_element_type=f32
        )
        collect(j)
    grads[span(last, block), :] = jnp.where(hits[span(last, block), :] > 0, slope, 0.0).astype(bf16)
    every(zs, drain)
    for n in range(1, zs):
        id_send(n).wait_send()

    coef = jnp.sum(dots[...], axis=1, keepdims=True) / (jnp.sum(norm[...], axis=1, keepdims=True) + 1e-06)
    enc_store = lambda j: pltpu.make_async_copy(
        enc_v.at[pl.ds(j * tile, tile)], enc_out.at[pl.ds(j * tile, tile)], out_sem.at[0, j]
    )
    dec_store = lambda j: pltpu.make_async_copy(dec_v.at[j], dec_out.at[:, pl.ds(j * tile, tile)], out_sem.at[1, j])
    def enc_all(j):
        enc_v[j * tile : (j + 1) * tile, :] = jnp.dot(
            x_turned[j], grads[...], preferred_element_type=f32
        ).astype(bf16)
        enc_store(j).start()

    def dec_all(j):
        dec_v[j] = (raw[j] - coef * dec_v[j].astype(f32)).astype(bf16)
        dec_store(j).start()

    def finish(j):
        dec_store(j).wait()
        enc_store(j).wait()

    [dec_all(j) for j in range(chunks)]
    [enc_all(j) for j in range(chunks)]
    [finish(j) for j in range(chunks)]


def crossed_plan(activations, block_lists, top_positions, enc_weight, enc_bias, dec_weight, dec_bias):
    token_count = activations.shape[0]
    block_rows, active_count = block_lists.shape
    group_rows = token_count // block_rows
    slot_count = max(2, 3 * token_count * active_count // (2 * group_rows * lax.axis_size(GROUP)))
    enc_grad, dec_grad = route_rows(
        activations, top_positions.T, block_lists.T, enc_weight, enc_bias, dec_weight, dec_bias,
        slot_count * group_rows, 768, 3, 1,
    )
    return (enc_grad, dec_grad)


def on_device(activations, block_lists, top_positions, *weights):
    rows, width = activations.shape
    feat_block = weights[0].shape[1]
    square = lax.axis_size("tok") == 4 and lax.axis_size("feat") == 4
    even = rows % 128 == 0 and width % 3072 == 0 and feat_block % 256 == 0 and 2 * top_positions.shape[1] == 128
    if square and even and lax.axis_size(GROUP) * (feat_block // 256) < 256:
        return crossed_plan(activations, block_lists, top_positions, *weights)
    return routed_plan(activations, block_lists, top_positions, *weights)


def solution(mesh):
    placed = (
        P(("grp", "tok", "feat"), None),
        P(("grp", "tok", "feat"), None),
        P(("grp", "tok", "feat"), None),
        P(None, ("tok", "feat")),
        P(("tok", "feat")),
        P(("tok", "feat"), None),
        P(),
    )
    return jax.shard_map(
        on_device,
        mesh=mesh,
        in_specs=placed,
        out_specs=(P(None, ("grp", "tok", "feat")), P(("grp", "tok", "feat"), None)),
        check_vma=False,
    )
```

```python
import functools

import jax
import jax.numpy as jnp
from jax import lax
from jax.experimental import pallas as pl
from jax.experimental.pallas import tpu as pltpu
from jax.sharding import PartitionSpec as P


def dispatch_rows(send_x, send_rel):
    result = (
        lax.all_to_all(send_x, ("tok", "feat"), split_axis=0, concat_axis=0, tiled=True),
        lax.all_to_all(send_rel, ("tok", "feat"), split_axis=0, concat_axis=0, tiled=True),
    )
    return result


def return_partials(partial_value):
    result = lax.all_to_all(partial_value, ("tok", "feat"), split_axis=0, concat_axis=0, tiled=True)
    return result


def dispatch_errors(send_err):
    result = lax.all_to_all(send_err, ("tok", "feat"), split_axis=0, concat_axis=0, tiled=True)
    return result


def routed_plan(activations, block_lists, top_positions, enc_weight, enc_bias, dec_weight, dec_bias):
    owner_count = lax.axis_size(("tok", "feat"))
    token_count, model_width = activations.shape
    block_rows, active_count = block_lists.shape
    group_rows = token_count // block_rows
    feat_block = enc_weight.shape[1]
    top_count = top_positions.shape[1]
    slot_count = max(2, 3 * token_count * active_count // (2 * group_rows * owner_count))
    per_owner = slot_count * group_rows
    buffer_rows = owner_count * per_owner
    pair_count = block_rows * active_count
    pair_ids = block_lists.reshape(pair_count)
    pair_order = jnp.arange(pair_count, dtype=jnp.int32)
    earlier = (pair_ids[:, None] == pair_ids[None, :]) & (pair_order[None, :] < pair_order[:, None])
    pair_rank = jnp.sum(earlier.astype(jnp.int32), axis=1)
    lane_index = jnp.arange(group_rows, dtype=jnp.int32)
    target = (
        (pair_ids * per_owner + pair_rank * group_rows)[:, None] + lane_index[None, :]
    ).reshape(-1)
    source = ((pair_order // active_count * group_rows)[:, None] + lane_index[None, :]).reshape(-1)
    column = jnp.repeat(pair_order % active_count, group_rows)
    slot_index = jnp.arange(buffer_rows, dtype=jnp.int32)
    hit_bool = slot_index[:, None] == target[None, :]
    hit_float = hit_bool.astype(jnp.float32)
    place_float = jnp.sum(
        hit_float.reshape(buffer_rows, block_rows, active_count, group_rows), axis=2
    ).reshape(buffer_rows, token_count)
    place = place_float.astype(jnp.bfloat16)
    filled = jnp.sum(place_float, axis=1)
    send_x = jnp.dot(place, activations, preferred_element_type=jnp.float32).astype(jnp.bfloat16)
    offsets = top_positions[source] - column[:, None] * feat_block
    offsets = jnp.where((offsets >= 0) & (offsets < feat_block), offsets, feat_block)
    rel_float = (
        jnp.dot(hit_float, offsets.astype(jnp.float32), precision=lax.Precision.HIGHEST)
        + (1.0 - filled)[:, None] * feat_block
    )
    send_rel = rel_float.astype(jnp.int32)
    recv_x, recv_rel = dispatch_rows(
        send_x.reshape(owner_count, per_owner, model_width),
        send_rel.reshape(owner_count, per_owner, top_count),
    )
    recv_x = recv_x.reshape(buffer_rows, model_width)
    recv_rel = recv_rel.reshape(buffer_rows, top_count)
    feature_iota = jnp.arange(feat_block, dtype=jnp.int32)
    mask_bool = jnp.zeros((buffer_rows, feat_block), jnp.bool_)
    for begin in range(0, top_count, 8):
        piece = recv_rel[:, begin : begin + 8]
        mask_bool = mask_bool | jnp.any(piece[:, :, None] == feature_iota[None, None, :], axis=1)
    feat_mask = mask_bool.astype(jnp.float32)
    pre_acts = jnp.dot(recv_x, enc_weight, preferred_element_type=jnp.float32) + enc_bias
    code_vals = (feat_mask * pre_acts).astype(jnp.bfloat16)
    partial_value = jnp.dot(code_vals, dec_weight, preferred_element_type=jnp.float32).astype(
        jnp.bfloat16
    )
    returned = return_partials(partial_value.reshape(owner_count, per_owner, model_width)).reshape(
        buffer_rows, model_width
    )
    summed = lax.dot_general(
        place, returned, (((0,), (0,)), ((), ())), preferred_element_type=jnp.float32
    )
    residual = (summed + dec_bias - activations.astype(jnp.float32)).astype(jnp.bfloat16)
    send_err = jnp.dot(place, residual, preferred_element_type=jnp.float32).astype(jnp.bfloat16)
    recv_err = dispatch_errors(send_err.reshape(owner_count, per_owner, model_width)).reshape(
        buffer_rows, model_width
    )
    grad_codes = lax.dot_general(
        recv_err, dec_weight, (((1,), (1,)), ((), ())), preferred_element_type=jnp.float32
    )
    grad_pre = (feat_mask * grad_codes).astype(jnp.bfloat16)
    enc_grad = lax.dot_general(
        recv_x, grad_pre, (((0,), (0,)), ((), ())), preferred_element_type=jnp.float32
    ).astype(jnp.bfloat16)
    raw_grad = lax.dot_general(
        code_vals, recv_err, (((0,), (0,)), ((), ())), preferred_element_type=jnp.float32
    )
    dec_float = dec_weight.astype(jnp.float32)
    along_coef = jnp.sum(raw_grad * dec_float, axis=1) / (
        jnp.sum(dec_float * dec_float, axis=1) + 1e-06
    )
    dec_grad = (raw_grad - along_coef[:, None] * dec_float).astype(jnp.bfloat16)
    return (enc_grad, dec_grad)


GROUP = ("tok", "feat")


MESH = pl.DeviceIdType.MESH


def route_rows(x, positions, lists, enc_weight, enc_bias, dec_weight, dec_bias, cap, tile, early, collective_id):
    zs, mates = lax.axis_size("feat"), lax.axis_size("tok")
    rows, width = x.shape
    feat_block = enc_weight.shape[1]
    id_width = 2 * positions.shape[0]
    chunks = width // tile
    block = mates * cap
    away = block - cap
    total, staged = zs * block, zs * away
    bf16, f32 = jnp.bfloat16, jnp.float32
    vmem, hbm = pl.BlockSpec(memory_space=pltpu.VMEM), pl.BlockSpec(memory_space=pl.ANY)
    sem = lambda *lead: pltpu.SemaphoreType.DMA(lead)
    line_sems = [sem(2, zs, chunks), sem(zs, chunks), sem(mates - 1, zs, chunks), sem(mates - 1, zs, chunks)]
    return pl.pallas_call(
        functools.partial(route_kernel, zs, mates, cap, early),
        out_shape=[
            jax.ShapeDtypeStruct((width, feat_block), bf16),
            jax.ShapeDtypeStruct((feat_block, width), bf16),
        ],
        in_specs=[hbm, vmem, vmem, hbm, vmem, hbm, vmem],
        out_specs=[hbm, hbm],
        scratch_shapes=[
            pltpu.VMEM((zs, chunks, rows, tile), bf16),
            pltpu.VMEM((zs, rows, id_width), bf16),
            pltpu.VMEM((chunks, total, tile), bf16),
            pltpu.VMEM((total, id_width), bf16),
            pltpu.VMEM((chunks, staged, tile), bf16),
            pltpu.VMEM((staged, id_width), bf16),
            pltpu.VMEM((zs, rows, block), bf16),
            pltpu.VMEM((zs, block, rows), bf16),
            pltpu.VMEM((total, feat_block), bf16),
            pltpu.VMEM((total, feat_block), bf16),
            pltpu.VMEM((total, feat_block), bf16),
            pltpu.VMEM((chunks, staged, tile), bf16),
            pltpu.VMEM((chunks, total, tile), bf16),
            pltpu.VMEM((zs, chunks, rows, tile), bf16),
            pltpu.VMEM((zs + 1, chunks, rows, tile), bf16),
            pltpu.VMEM((zs, chunks, rows, tile), bf16),
            pltpu.VMEM((chunks, total, tile), bf16),
            pltpu.VMEM((width, feat_block), bf16),
            pltpu.VMEM((chunks, feat_block, tile), bf16),
            pltpu.VMEM((chunks, tile, total), bf16),
            pltpu.VMEM((feat_block, total), bf16),
            pltpu.VMEM((chunks, feat_block, tile), f32),
            pltpu.VMEM((feat_block, 128), f32),
            pltpu.VMEM((feat_block, 128), f32),
            pltpu.VMEM((id_width // 2, 128), f32),
            pltpu.VMEM((feat_block, 128), bf16),
        ]
        + line_sems
        + [sem(zs - 1), sem(zs - 1), sem(mates - 1, zs), sem(mates - 1, zs)]
        + line_sems
        + [sem(mates - 1, zs, chunks), sem(mates - 1, zs, chunks), sem(zs, chunks), sem(zs + 1, chunks)]
        + [sem(1), sem(chunks), sem(chunks), sem(2, chunks)],
        compiler_params=pltpu.CompilerParams(
            collective_id=collective_id, has_side_effects=True, vmem_limit_bytes=62 * 1024 * 1024
        ),
        name="route_rows",
    )(x, positions, lists, enc_weight, enc_bias.reshape(1, feat_block), dec_weight, dec_bias.reshape(chunks, 1, tile))


def route_kernel(
    zs, mates, cap, early, x_ref, position_ref, list_ref, enc_ref, ebias_ref, dec_ref, dbias_ref, enc_out, dec_out,
    x_line, id_line, x_in, id_in, stage, id_stage, spread, pick, codes, hits, grads,
    p_stage, p_in, c_out, c_in, r_line, r_in, enc_v, dec_v, x_turned, codes_turned, raw, norm, dots, keys, marks,
    xl_send, xl_recv, xm_send, xm_recv, il_send, il_recv, im_send, im_recv,
    rl_send, rl_recv, rm_send, rm_recv, pm_send, pm_recv, c_send, c_recv,
    once, own_sem, dec_sem, out_sem,
):
    rows, width = x_ref.shape
    chunks, _, tile = dec_v.shape
    feat_block = enc_v.shape[1]
    block, away = mates * cap, (mates - 1) * cap
    tops = position_ref.shape[0]
    parts = feat_block // 256
    bf16, f32 = jnp.bfloat16, jnp.float32
    me, z = lax.axis_index("tok"), lax.axis_index("feat")

    def mate(m):
        return {"tok": lax.rem(me + m + mates, mates)}

    def along(k):
        return {"feat": jnp.minimum(jnp.maximum(z + 1 - 2 * k, 0), zs - 1)}

    def onward(k):
        return (z + 1 - 2 * k >= 0) & (z + 1 - 2 * k < zs)

    def span(zb, size, offset=0, length=None):
        return pl.ds(pl.multiple_of(zb * size + offset, 16), length or size)

    def remote(src, dst, send, recv, where):
        return pltpu.make_async_remote_copy(
            src_ref=src, dst_ref=dst, send_sem=send, recv_sem=recv, device_id=where, device_id_type=MESH
        )

    def line(ref, send, recv, k, zb, j, src=None):
        here = ref.at[zb, j]
        return remote(here if src is None else src, here, send.at[k, zb, j], recv.at[zb, j], along(k))

    def id_send(n):
        return remote(
            id_line.at[z], id_line.at[z], il_send.at[n - 1], il_recv.at[n - 1], {"feat": lax.rem(z + n, zs)}
        )

    def id_mate(m, zb):
        return remote(
            id_stage.at[span(zb, away, (m - 1) * cap, cap)], id_in.at[span(zb, block, m * cap, cap)],
            im_send.at[m - 1, zb], im_recv.at[m - 1, zb], mate(m),
        )

    def to_mate(src, dst, send, recv, m, zb, j, sign=1):
        return remote(
            src.at[j, span(zb, away, (m - 1) * cap, cap)], dst.at[j, span(zb, block, m * cap, cap)],
            send.at[m - 1, zb, j], recv.at[m - 1, zb, j], mate(sign * m),
        )

    x_mate = functools.partial(to_mate, stage, x_in, xm_send, xm_recv)
    r_mate = functools.partial(to_mate, stage, r_in, rm_send, rm_recv)
    p_mate = functools.partial(to_mate, p_stage, p_in, pm_send, pm_recv, sign=-1)

    def chain(k, zz, j):
        slot = zz + 1 - k
        return remote(c_out.at[zz, j], c_in.at[slot, j], c_send.at[zz, j], c_recv.at[slot, j], along(k))

    def every(count, body):
        def step(i, carry):
            body(i)
            return carry

        lax.fori_loop(0, count, step, 0)

    def others(body):
        for m in range(1, mates):
            body(m)

    def at_distance(d, body):
        if d == 0:
            body(z, None)
        else:

            def side(k):
                zb = z - d + 2 * d * k
                pl.when((zb >= 0) & (zb < zs))(lambda: body(zb, k))

            every(2, side)

    cols = lambda j: pl.ds(pl.multiple_of(j * tile, tile), tile)
    own_load = lambda j: pltpu.make_async_copy(x_ref.at[:, cols(j)], x_line.at[z, j], own_sem.at[j])
    dec_load = lambda j: pltpu.make_async_copy(dec_ref.at[:, cols(j)], dec_v.at[j], dec_sem.at[j])
    enc_load = pltpu.make_async_copy(enc_ref, enc_v, once.at[0])
    every(chunks, lambda j: own_load(j).start())
    enc_load.start()
    every(chunks, lambda j: dec_load(j).start())
    barrier = pltpu.get_barrier_semaphore()
    others(lambda m: pl.semaphore_signal(barrier, inc=1, device_id=mate(m), device_id_type=MESH))
    for n in range(1, zs):
        pl.semaphore_signal(barrier, inc=1, device_id={"feat": lax.rem(z + n, zs)}, device_id_type=MESH)
    def plan(zb):
        halves = id_line[zb][:, :tops].astype(f32)
        lane = lax.broadcasted_iota(jnp.int32, (rows, block), 1)
        low = lax.broadcasted_iota(jnp.int32, (rows, rows), 0) > lax.broadcasted_iota(jnp.int32, (rows, rows), 1)
        low = jnp.where(low, 1.0, 0.0).astype(bf16)
        named = jnp.zeros((rows, block), f32)
        for m in range(mates):
            owner = lax.rem(me + m, mates) * zs + z
            first = (parts * owner + 1).astype(f32)
            hit = jnp.where((halves >= first) & (halves < first + parts), 1.0, 0.0)
            hit = jnp.max(hit, axis=1, keepdims=True)
            named = jnp.where((lane >= m * cap) & (lane < (m + 1) * cap), hit, named)
        before = jnp.dot(low, named.astype(bf16), preferred_element_type=f32).astype(jnp.int32)
        slot = lax.rem(lane, cap)
        put = jnp.where((before == slot) & (named > 0), 1.0, 0.0)
        spread[zb] = put.astype(bf16)
        pick[zb] = put.T.astype(bf16)

    def picked(zb, values):
        return jnp.dot(pick[zb], values, preferred_element_type=f32).astype(bf16)

    def share_ids(zb):
        out = picked(zb, id_line[zb])
        id_in[span(zb, block, 0, cap), :] = out[:cap]
        id_stage[span(zb, away), :] = out[cap:]
        others(lambda m: id_mate(m, zb).start())

    def gather_ids():
        def other(n):
            id_send(n).wait_recv()
            zb = lax.rem(z - n + zs, zs)
            plan(zb)
            share_ids(zb)

        for n in range(1, zs):
            other(n)

    def hand_out(ref, dst, send_to, zb, j):
        out = picked(zb, ref[zb, j])
        dst[j, span(zb, block, 0, cap), :] = out[:cap]
        stage[j, span(zb, away), :] = out[cap:]
        others(lambda m: send_to(m, zb, j).start())

    def gather_one(ref, send, recv, dst, send_to, zb, k, j, own=False):
        if not own:
            line(ref, send, recv, k, zb, j).wait_recv()
            pl.when(onward(k))(lambda: line(ref, send, recv, k, zb, j).start())
        hand_out(ref, dst, send_to, zb, j)

    def gather(one, d, begin=0, end=chunks):
        every(end - begin, lambda i: at_distance(d, lambda zb, k: one(zb, k, begin + i)))

    x_one = functools.partial(gather_one, x_line, xl_send, xl_recv, x_in, x_mate)
    r_one = functools.partial(gather_one, r_line, rl_send, rl_recv, r_in, r_mate)
    gather_x, gather_r = functools.partial(gather, x_one), functools.partial(gather, r_one)
    mine = (me * zs + z).astype(f32)
    strip = 64
    late = chunks - early

    def mark(g):
        at = pl.ds(pl.multiple_of(g * 128, 128), 128)
        turned = id_in[at, :].astype(f32).T
        keys[...] = (turned[:tops] - (1.0 + parts * mine)) * 256.0 + turned[tops:]

        def part(i):
            feature = (lax.broadcasted_iota(jnp.int32, (strip, 128), 0) + i * strip).astype(f32)
            found = jnp.zeros((strip, 128), f32)
            for t in range(tops):
                found = jnp.where(keys[t : t + 1, :] == feature, 1.0, found)
            marks[pl.ds(pl.multiple_of(i * strip, strip), strip), :] = found.astype(bf16)

        every(feat_block // strip, part)
        hits[at, :] = marks[...].T

    def encode(zb):
        pre = jnp.zeros((block, feat_block), f32)
        for j in range(chunks):
            others(lambda m: x_mate(m, zb, j).wait_recv())
            pre += jnp.dot(
                x_in[j, span(zb, block), :], enc_v[j * tile : (j + 1) * tile, :], preferred_element_type=f32
            )
        code = jnp.where(hits[span(zb, block), :] > 0, pre + ebias_ref[...], 0.0).astype(bf16)
        codes[span(zb, block), :] = code

    def decode(zb, part):
        def chunk(i):
            j = part * early + i
            out = jnp.dot(codes[span(zb, block), :], dec_v[j], preferred_element_type=f32).astype(bf16)
            p_in[j, span(zb, block, 0, cap), :] = out[:cap]
            p_stage[j, span(zb, away), :] = out[cap:]
            others(lambda m: p_mate(m, zb, j).start())

        every(late if part else early, chunk)

    def merged(zz, j):
        others(lambda m: p_mate(m, zz, j).wait_recv())
        return jnp.dot(spread[zz], p_in[j, span(zz, block), :], preferred_element_type=f32)

    def row_of(i):
        turn = jnp.where(z < zs // 2, 1 + i, zs - 1 - i)
        return lax.rem(z + turn, zs)

    def pass_chunk(i, j):
        zz = row_of(i)
        k = jnp.where(zz > z, 0, 1)
        first = jnp.where(zz > z, z == 0, z == zs - 1)

        @pl.when(first)
        def _():
            c_out[zz, j] = merged(zz, j).astype(bf16)

        @pl.when(jnp.logical_not(first))
        def _():
            chain(k, zz, j).wait_recv()
            c_out[zz, j] = (merged(zz, j) + c_in[zz + 1 - k, j].astype(f32)).astype(bf16)

        chain(k, zz, j).start()

    def pass_on(i, part):
        every(late if part else early, lambda c: pass_chunk(i, part * early + c))

    def settle(j):
        raw[0, :rows, :] = (
            merged(z, j) + dbias_ref[j] - x_line[z, j].astype(f32)
        )
        for k in range(2):

            @pl.when(onward(1 - k))
            def _():
                chain(k, z, j).wait_recv()
                raw[0, :rows, :] += c_in[z + 1 - k, j].astype(f32)

        r_line[z, j] = raw[0, :rows, :].astype(bf16)
        for k in range(2):
            pl.when(onward(k))(lambda: line(r_line, rl_send, rl_recv, k, z, j).start())
        hand_out(r_line, r_in, r_mate, z, j)

    def arrived(zb, begin, end):
        every(end - begin, lambda i: others(lambda m: r_mate(m, zb, begin + i).wait_recv()))

    def slopes(zb):
        slope = jnp.zeros((block, feat_block), f32)
        for j in range(chunks):
            slope += lax.dot_general(
                r_in[j, span(zb, block), :], dec_v[j], (((1,), (1,)), ((), ())), preferred_element_type=f32
            )
        grads[span(zb, block), :] = jnp.where(hits[span(zb, block), :] > 0, slope, 0.0).astype(bf16)

    def folded(values):
        return sum(values[:, n * 128 : (n + 1) * 128] for n in range(tile // 128))

    def weigh(j):
        dec = dec_v[j].astype(f32)
        norm[...] += folded(dec * dec)

    def collect(j):
        value = jnp.dot(codes_turned[...], r_in[j], preferred_element_type=f32)
        raw[j] = value
        dots[...] += folded(value * dec_v[j].astype(f32))

    def drain(zb):
        def sent(send_line, send_mate, j):
            for k in range(2):
                came = (zb <= z) if k == 0 else (zb >= z)
                pl.when(onward(k) & came)(lambda: send_line(k, zb, j).wait_send())
            if send_mate is not None:
                others(lambda m: send_mate(m, zb, j).wait_send())

        def chunk(j):
            sent(functools.partial(line, x_line, xl_send, xl_recv), None, j)
            sent(functools.partial(line, r_line, rl_send, rl_recv), r_mate, j)
            others(lambda m: p_mate(m, zb, j).wait_send())
            pl.when(zb != z)(lambda: chain(0, zb, j).wait_send())

        every(chunks, chunk)
        others(lambda m: id_mate(m, zb).wait_send())

    at_end = (z == 0) | (z == zs - 1)
    inside = jnp.logical_not(at_end)

    def own_ids():
        groups = list_ref.shape[1]
        token = lax.broadcasted_iota(jnp.int32, (groups, rows), 1) // (rows // groups)
        wide = jnp.where(token == lax.broadcasted_iota(jnp.int32, (groups, rows), 0), 1.0, 0.0).astype(bf16)
        lists = jnp.dot(list_ref[...].astype(f32).astype(bf16), wide, preferred_element_type=f32)
        position = position_ref[...]
        column, within = position // feat_block, position % feat_block
        chosen = jnp.zeros((tops, rows), f32)
        for k in range(list_ref.shape[0]):
            chosen = jnp.where(column == k, lists[k : k + 1, :], chosen)
        first = chosen * parts + (within // 256 + 1).astype(f32)
        pair = jnp.concatenate([first, (within % 256).astype(f32)], axis=0)
        id_line[z] = pair.T.astype(bf16)

    own_ids()
    plan(z)
    pl.semaphore_wait(barrier, mates + zs - 2)
    for n in range(1, zs):
        id_send(n).start()

    for k in range(2):

        @pl.when(onward(k))
        def _():
            every(chunks, lambda j: line(x_line, xl_send, xl_recv, k, z, j, x_ref.at[:, cols(j)]).start())

    share_ids(z)
    def own_x(j):
        own_load(j).wait()
        x_one(z, None, j, own=True)

    every(early, own_x)
    gather_ids()
    every(late, lambda i: own_x(early + i))
    gather_x(1)
    for m in range(1, mates):
        every(zs, lambda zb: id_mate(m, zb).wait_recv())
    every(zs * block // 128, mark)
    enc_load.wait()
    every(chunks, lambda j: dec_load(j).wait())

    @pl.when(at_end)
    def _():
        gather_x(2, 0, 1)
        encode(row_of(0))
        decode(row_of(0), 0)
        gather_x(2, 1)
        pass_on(0, 0)
        gather_x(3, 0, 1)
        encode(row_of(1))
        decode(row_of(1), 0)
        gather_x(3, 1)
        pass_on(1, 0)
        encode(z)
        decode(z, 0)
        encode(row_of(2))
        decode(row_of(2), 0)

    @pl.when(inside)
    def _():
        gather_x(2)

        encode(row_of(0))
        decode(row_of(0), 0)
        encode(z)
        decode(z, 0)
        encode(row_of(1))
        decode(row_of(1), 0)
        encode(row_of(2))
        decode(row_of(2), 0)

    @pl.when(at_end)
    def _():
        decode(row_of(0), 1)
        decode(row_of(1), 1)
        decode(row_of(2), 1)
        decode(z, 1)

    @pl.when(inside)
    def _():
        decode(row_of(0), 1)
        decode(z, 1)
        decode(row_of(1), 1)
        decode(row_of(2), 1)

    norm[...] = jnp.zeros(norm.shape, f32)
    dots[...] = jnp.zeros(dots.shape, f32)
    every(chunks, weigh)

    def turn(j):
        x_turned[j] = x_in[j].T

    every(chunks, turn)
    codes_turned[...] = codes[...].T
    every(zs, lambda zb: every(chunks, lambda j: others(lambda m: x_mate(m, zb, j).wait_send())))
    below = z < zs // 2
    inner, inner_way = jnp.where(below, z + 1, z - 1), jnp.where(below, 1, 0)
    outer, outer_way = jnp.where(below, z - 1, z + 1), jnp.where(below, 0, 1)

    @pl.when(at_end)
    def _():
        pass_on(2, 0)
        pass_on(0, 1)
        pass_on(1, 1)
        gather_r(1, 0, early)
        pass_on(2, 1)
        every(early, settle)
        gather_r(2, 0, early)
        gather_r(1, early)
        every(late, lambda i: settle(early + i))
        gather_r(2, early)
        gather_r(3)

    @pl.when(inside)
    def _():
        pass_on(0, 0)
        every(early, settle)
        every(early, lambda i: r_one(inner, inner_way, i))
        pass_on(1, 0)
        pass_on(2, 0)
        pass_on(0, 1)
        pass_on(1, 1)
        every(late, lambda i: settle(early + i))
        pass_on(2, 1)
        every(early, lambda i: r_one(outer, outer_way, i))
        every(late, lambda i: r_one(inner, inner_way, early + i))
        gather_r(2, 0, early)
        every(late, lambda i: r_one(outer, outer_way, early + i))
        gather_r(2, early)

    last = jnp.where(at_end, row_of(2), row_of(1))

    def whole(zb):
        arrived(zb, 0, chunks)
        slopes(zb)

    whole(z)
    whole(row_of(0))
    whole(jnp.where(at_end, row_of(1), row_of(2)))
    slope = jnp.zeros((block, feat_block), f32)
    for j in range(chunks):
        arrived(last, j, j + 1)
        slope += lax.dot_general(
            r_in[j, span(last, block), :], dec_v[j], (((1,), (1,)), ((), ())), preferred_element_type=f32
        )
        collect(j)
    grads[span(last, block), :] = jnp.where(hits[span(last, block), :] > 0, slope, 0.0).astype(bf16)

    coef = jnp.sum(dots[...], axis=1, keepdims=True) / (jnp.sum(norm[...], axis=1, keepdims=True) + 1e-06)
    enc_store = lambda j: pltpu.make_async_copy(
        enc_v.at[pl.ds(j * tile, tile)], enc_out.at[pl.ds(j * tile, tile)], out_sem.at[0, j]
    )
    dec_store = lambda j: pltpu.make_async_copy(dec_v.at[j], dec_out.at[:, pl.ds(j * tile, tile)], out_sem.at[1, j])
    def enc_all(j):
        enc_v[j * tile : (j + 1) * tile, :] = jnp.dot(
            x_turned[j], grads[...], preferred_element_type=f32
        ).astype(bf16)
        enc_store(j).start()

    def dec_all(j):
        dec_v[j] = (raw[j] - coef * dec_v[j].astype(f32)).astype(bf16)
        dec_store(j).start()

    def finish(j):
        dec_store(j).wait()
        enc_store(j).wait()

    [dec_all(j) for j in range(chunks)]
    [enc_all(j) for j in range(chunks)]
    every(zs, drain)
    for n in range(1, zs):
        id_send(n).wait_send()
    [finish(j) for j in range(chunks)]


def crossed_plan(activations, block_lists, top_positions, enc_weight, enc_bias, dec_weight, dec_bias):
    token_count = activations.shape[0]
    block_rows, active_count = block_lists.shape
    group_rows = token_count // block_rows
    slot_count = max(2, 3 * token_count * active_count // (2 * group_rows * lax.axis_size(GROUP)))
    enc_grad, dec_grad = route_rows(
        activations, top_positions.T, block_lists.T, enc_weight, enc_bias, dec_weight, dec_bias,
        slot_count * group_rows, 768, 3, 1,
    )
    return (enc_grad, dec_grad)


def on_device(activations, block_lists, top_positions, *weights):
    rows, width = activations.shape
    feat_block = weights[0].shape[1]
    square = lax.axis_size("tok") == 4 and lax.axis_size("feat") == 4
    even = rows % 128 == 0 and width % 3072 == 0 and feat_block % 256 == 0 and 2 * top_positions.shape[1] == 128
    if square and even and lax.axis_size(GROUP) * (feat_block // 256) < 256:
        return crossed_plan(activations, block_lists, top_positions, *weights)
    return routed_plan(activations, block_lists, top_positions, *weights)


def solution(mesh):
    placed = (
        P(("grp", "tok", "feat"), None),
        P(("grp", "tok", "feat"), None),
        P(("grp", "tok", "feat"), None),
        P(None, ("tok", "feat")),
        P(("tok", "feat")),
        P(("tok", "feat"), None),
        P(),
    )
    return jax.shard_map(
        on_device,
        mesh=mesh,
        in_specs=placed,
        out_specs=(P(None, ("grp", "tok", "feat")), P(("grp", "tok", "feat"), None)),
        check_vma=False,
    )
```
